32 devices in a mesh: gx: 4 (over y, core), gy: 4 (over z), gz: 2 (over x).
Axes of the slice: x: 2, y: 2, z: 4, core: 2. Of those that a mesh axis runs over, the one named last changes fastest.
Arguments:
- stiffness: float32 [32, 48, 256], P('gx', 'gy', 'gz'), may hold values from 0.5 to 5
- density: float32 [32, 48, 256], P('gx', 'gy', 'gz'), may hold values from 1 to 4
- load: float32 [3, 32, 48, 256], P(None, 'gx', 'gy', 'gz'), may hold values from -6 to 6
- alive: int32 [4, 32, 48, 256], P(None, 'gx', 'gy', 'gz'), may hold values 0 or 1
- surf_coords: float32 [512, 3, 128], P(('gx', 'gy', 'gz')), may hold values from 0 to 1
- surf_nodes: int32 [512, 128], P(('gx', 'gy', 'gz')), may hold values from 0 to 12287
- routes: int32 [4, 512], P(None, ('gx', 'gy', 'gz')), may hold values from 0 to 1, as said below
- pairs: int32 [4, 32, 64, 2], P(None, ('gx', 'gy', 'gz')), may hold values from 0 to 15, as said below
Outputs:
- element_velocity: float32 [3, 32, 48, 256], P(None, 'gx', 'gy', 'gz')
- element_stress: float32 [6, 32, 48, 256], P(None, 'gx', 'gy', 'gz')
The draws below stay inside these ranges and needn't reach their ends.
Inputs may be any that keep to these rules, and one draw needn't show every extreme that they name: `routes`: in every step a device sends at most 8 of its blocks to one box, and all devices of a gz column send exactly 8 blocks to one common box of that column. `pairs`: every slot named is live at that box and step whenever the box holds a block at all.
All inputs are finite; a program needn't handle non-finite values. No bound on the sum of `alive` on one device may be relied on, other than what follows from the above.
Results may differ from the reference program's by a relative error of at most 0.0003.
Values sent between devices are 32-bit elements; how exact they have to be, the bound alone decides.
A program may use at most 64 MiB of HBM per device.

```python
import math
import jax
import jax.numpy as jnp
from jax import lax

CX = 8
CY = 12
CZ = 128
SB = 16
NPAIR = 64
BNODES = 128
STEPS = 4
NX = 32
NY = 48
NZ = 256
BLOCKS = 512
N_GX = 4
N_GY = 4
N_GZ = 2


def contact_plan(key):
    devices = N_GX * N_GY * N_GZ
    columns = N_GX * N_GY
    capacity = max(SB // 4, SB // N_GZ)
    entries = N_GZ * capacity
    key_target = jax.random.fold_in(key, 101)
    key_noise = jax.random.fold_in(key, 202)
    key_shuffle = jax.random.fold_in(key, 303)
    key_picks = jax.random.fold_in(key, 404)
    target = jax.random.randint(key_target, (STEPS, columns), 0, N_GZ)
    target_device = jnp.repeat(target, N_GZ, axis=1)
    entry = jnp.arange(entries, dtype=jnp.int32)
    entry_box = entry // capacity
    noise = jax.random.randint(key_noise, (STEPS, devices, entries), 0, 65536)
    score = jnp.where(entry_box[None, None, :] == target_device[:, :, None], 0, 1 + noise) * entries + entry
    order = jnp.argsort(score, axis=-1)
    chosen = entry_box[order[..., :SB]]
    shuffle = jax.random.randint(key_shuffle, (STEPS, devices, SB), 0, 65536) * SB + jnp.arange(SB, dtype=jnp.int32)
    placing = jnp.argsort(shuffle, axis=-1)
    route_table = jnp.take_along_axis(chosen, placing, axis=-1)
    counts = jnp.sum((route_table[..., None] == jnp.arange(N_GZ, dtype=jnp.int32)).astype(jnp.int32), axis=2)
    counts = counts.reshape(STEPS, columns, N_GZ, N_GZ).transpose(0, 1, 3, 2).reshape(STEPS, devices, N_GZ)
    live = jnp.arange(capacity, dtype=jnp.int32)[None, None, None, :] < counts[..., None]
    live = live.reshape(STEPS, devices, entries)
    live_first = jnp.argsort(jnp.where(live, 0, 1) * entries + entry, axis=-1)
    how_many = jnp.maximum(jnp.sum(live.astype(jnp.int32), axis=-1), 1)
    picks = jax.random.randint(key_picks, (STEPS, devices, NPAIR * 2), 0, 65536) % how_many[..., None]
    slot_table = jnp.take_along_axis(live_first, picks, axis=-1).reshape(STEPS, devices, NPAIR, 2)
    return (route_table.reshape(STEPS, devices * SB).astype(jnp.int32), slot_table.astype(jnp.int32))


def draw_routes(key, part):
    return contact_plan(key)[0]


def draw_pairs(key, part):
    return contact_plan(key)[1]


def plant(values, own_key, smallest, top_value):
    place = [jax.random.randint(jax.random.fold_in(own_key, axis), (), 0, length) for axis, length in enumerate(values.shape)]
    widest = values.shape.index(max(values.shape))
    next_to = place[:widest] + [(place[widest] + 1) % values.shape[widest]] + place[widest + 1:]
    return values.at[tuple(place)].set(smallest).at[tuple(next_to)].set(top_value)


def shard_levels(stream_key, dims, split, least, top_value):
    def one(axis_at, blocks):
        draws = jax.random.uniform(jax.random.fold_in(jax.random.fold_in(stream_key, 6), axis_at), (blocks,), jnp.float32, least / len(split), top_value / len(split))
        return jnp.repeat(jnp.exp(draws), dims[axis_at] // blocks).reshape((-1,) + (1,) * (len(dims) - axis_at - 1))

    loudness = one(*split[0])
    for cut in split[1:]:
        loudness = loudness * one(*cut)
    return loudness


def scatter_about(stream_key, extent, spread, bound, cuts=(), kind=jnp.bfloat16):
    array = spread * jax.random.normal(stream_key, extent, jnp.float32)
    if cuts:
        array = array * shard_levels(stream_key, extent, cuts, -0.22, 0.18)
    return jnp.clip(array, -bound, bound).astype(kind)


def setup_inputs(seed: int = 0) -> dict:
    key_of = jax.random.split(jax.random.key(seed), 9)
    stiffness = jnp.clip(jnp.exp(math.log(5.0) - 2.3025851 * jax.random.uniform(key_of[0], (NX, NY, NZ), jnp.float32) ** shard_levels(key_of[0], (NX, NY, NZ), ((0, 4), (1, 4), (2, 2)), -0.2, 0.2)), 0.5, 5.0)
    density = jnp.clip(jnp.exp(math.log(4.0) - 1.3862944 * jax.random.uniform(key_of[1], (NX, NY, NZ), jnp.float32) ** shard_levels(key_of[1], (NX, NY, NZ), ((0, 4), (1, 4), (2, 2)), -0.2, 0.2)), 1.0, 4.0)
    load = scatter_about(key_of[2], (3, NX, NY, NZ), 1.0, 6.0, ((1, 4), (2, 4), (3, 2)), jnp.float32)
    alive = plant((jax.random.randint(key_of[3], (STEPS, NX, NY, NZ), 0, 10) < 9).astype(jnp.int32), jax.random.fold_in(key_of[3], 1), 0, 1)
    surf_coords = jnp.clip(1.0 * jax.random.uniform(key_of[4], (BLOCKS, 3, BNODES), jnp.float32) ** shard_levels(key_of[4], (BLOCKS, 3, BNODES), ((0, 32),), -0.2, 0.2), 0.0, 1.0)
    surf_nodes = plant(jax.random.randint(key_of[5], (BLOCKS, BNODES), 0, CX * CY * CZ), jax.random.fold_in(key_of[5], 1), 0, (CX * CY * CZ) - 1).astype(jnp.int32)
    routes = draw_routes(jax.random.fold_in(key_of[8], 71), 0)
    pairs = draw_pairs(jax.random.fold_in(key_of[8], 71), 0)
    return dict(stiffness=stiffness, density=density, load=load, alive=alive, surf_coords=surf_coords, surf_nodes=surf_nodes, routes=routes, pairs=pairs)


REPULSION = 1.0
KERNEL_SCALE = 0.08
TIME_STEP = 0.2
HIGHEST = lax.Precision.HIGHEST
CORNERS = [(0, 0, 0), (0, 0, 1), (0, 1, 0), (0, 1, 1), (1, 0, 0), (1, 0, 1), (1, 1, 0), (1, 1, 1)]


def corner(field, offsets):
    size_x = field.shape[1] - 1
    size_y = field.shape[2] - 1
    size_z = field.shape[3] - 1
    return field[:, offsets[0]:offsets[0] + size_x, offsets[1]:offsets[1] + size_y, offsets[2]:offsets[2] + size_z]


def element_stress(disp, modulus):
    grads = []
    for axis in range(3):
        parts = []
        for first in (0, 1):
            for second in (0, 1):
                upper = [first, second]
                upper.insert(axis, 1)
                lower = [first, second]
                lower.insert(axis, 0)
                parts.append(corner(disp, upper) - corner(disp, lower))
        grads.append(0.25 * (parts[0] + parts[1] + parts[2] + parts[3]))
    strain_xx = grads[0][0]
    strain_yy = grads[1][1]
    strain_zz = grads[2][2]
    strain_xy = 0.5 * (grads[1][0] + grads[0][1])
    strain_yz = 0.5 * (grads[2][1] + grads[1][2])
    strain_zx = 0.5 * (grads[0][2] + grads[2][0])
    trace = strain_xx + strain_yy + strain_zz
    return jnp.stack([modulus * (2.0 * strain_xx + trace), modulus * (2.0 * strain_yy + trace),
                      modulus * (2.0 * strain_zz + trace), modulus * 2.0 * strain_xy,
                      modulus * 2.0 * strain_yz, modulus * 2.0 * strain_zx])


def node_forces(stress, load):
    rows = ((stress[0], stress[3], stress[5]), (stress[3], stress[1], stress[4]), (stress[5], stress[4], stress[2]))
    total = jnp.float32(0.0)
    for offsets in CORNERS:
        signs = [2.0 * offsets[0] - 1.0, 2.0 * offsets[1] - 1.0, 2.0 * offsets[2] - 1.0]
        pieces = []
        for index in range(3):
            row = rows[index]
            pieces.append(-0.25 * (signs[0] * row[0] + signs[1] * row[1] + signs[2] * row[2]) + 0.125 * load[index])
        term = jnp.stack(pieces)
        total = total + jnp.pad(term, ((0, 0), (offsets[0], 1 - offsets[0]), (offsets[1], 1 - offsets[1]), (offsets[2], 1 - offsets[2])))
    return total


def node_mass(density):
    share = 0.125 * density
    total = jnp.float32(0.0)
    for offsets in CORNERS:
        total = total + jnp.pad(share, ((offsets[0], 1 - offsets[0]), (offsets[1], 1 - offsets[1]), (offsets[2], 1 - offsets[2])))
    return total


def element_mean(vel):
    total = jnp.float32(0.0)
    for offsets in CORNERS:
        total = total + corner(vel, offsets)
    return 0.125 * total


def selection(route_row, boxes, capacity):
    hits = route_row[None, :] == boxes[:, None]
    rank = jnp.cumsum(hits.astype(jnp.int32), axis=1) - 1
    chosen = hits[:, None, :] & (rank[:, None, :] == jnp.arange(capacity, dtype=jnp.int32)[None, :, None])
    return chosen.astype(jnp.float32)


def pair_forces(first, second, valid_first, valid_second):
    diff = first[:, :, :, None] - second[:, :, None, :]
    dist = jnp.sum(diff * diff, axis=1)
    weight = REPULSION * jnp.exp(-dist / KERNEL_SCALE) * (valid_first * valid_second)[:, None, None]
    return jnp.sum(diff * weight[:, None, :, :], axis=3)


def owner_forces(received, valid, pair_list):
    first = received[pair_list[:, 0]]
    second = received[pair_list[:, 1]]
    forces = pair_forces(first, second, valid[pair_list[:, 0]], valid[pair_list[:, 1]])
    onehot = (pair_list[:, 0][:, None] == jnp.arange(received.shape[0], dtype=jnp.int32)[None, :]).astype(jnp.float32)
    return jnp.einsum('pk,pxn->kxn', onehot, forces, precision=HIGHEST)


def reference(stiffness, density, load, alive, surf_coords, surf_nodes, routes, pairs):
    devices = N_GX * N_GY * N_GZ
    columns = N_GX * N_GY
    capacity = max(SB // 4, SB // N_GZ)
    nodes_shape = (3, NX + 1, NY + 1, NZ + 1)
    mass = node_mass(density)
    disp = jnp.zeros(nodes_shape, jnp.float32)
    vel = jnp.zeros(nodes_shape, jnp.float32)
    earlier = disp
    owner = jnp.arange(BLOCKS, dtype=jnp.int32) // SB
    index_x = owner // (N_GY * N_GZ)
    index_y = (owner // N_GZ) % N_GY
    index_z = owner % N_GZ
    local_i = surf_nodes // (CY * CZ)
    local_j = (surf_nodes // CZ) % CY
    local_k = surf_nodes % CZ
    global_i = index_x[:, None] * CX + local_i
    global_j = index_y[:, None] * CY + local_j
    global_k = index_z[:, None] * CZ + local_k
    flat_ids = (global_i * (NY + 1) + global_j) * (NZ + 1) + global_k
    boxes = jnp.arange(N_GZ, dtype=jnp.int32)
    for step in range(STEPS):
        lagged = earlier.reshape(3, -1)
        positions = jnp.moveaxis(lagged[:, flat_ids], 0, 1) + surf_coords
        positions = positions.reshape(devices, SB, 3, BNODES)
        route_rows = routes[step].reshape(devices, SB)
        chosen = jax.vmap(lambda row: selection(row, boxes, capacity))(route_rows)
        send = jnp.einsum('dbks,dsxn->dbkxn', chosen, positions, precision=HIGHEST)
        valid = jnp.sum(chosen, axis=3)
        send = send.reshape(columns, N_GZ, N_GZ, capacity, 3, BNODES).transpose(0, 2, 1, 3, 4, 5)
        send = send.reshape(devices, N_GZ * capacity, 3, BNODES)
        valid = valid.reshape(columns, N_GZ, N_GZ, capacity).transpose(0, 2, 1, 3).reshape(devices, N_GZ * capacity)
        slot_force = lax.map(lambda item: owner_forces(item[0], item[1], item[2]), (send, valid, pairs[step]))
        back = slot_force.reshape(columns, N_GZ, N_GZ, capacity, 3, BNODES).transpose(0, 2, 1, 3, 4, 5)
        back = back.reshape(devices, N_GZ, capacity, 3, BNODES)
        block_force = jnp.einsum('dbks,dbkxn->dsxn', chosen, back, precision=HIGHEST)
        block_force = jnp.moveaxis(block_force.reshape(BLOCKS, 3, BNODES), 1, 0)
        contact = jnp.zeros((3, lagged.shape[1]), jnp.float32).at[:, flat_ids].add(block_force)
        modulus = stiffness * alive[step].astype(jnp.float32)
        force = node_forces(element_stress(disp, modulus), load) + contact.reshape(nodes_shape)
        vel = vel + TIME_STEP * force / mass[None]
        earlier = disp
        disp = disp + TIME_STEP * vel
    final_modulus = stiffness * alive[STEPS - 1].astype(jnp.float32)
    return element_mean(vel), element_stress(disp, final_modulus)
```

```python
import functools
import itertools
import math

import jax
import jax.numpy as jnp
from jax import lax
from jax.experimental import pallas as pl
from jax.experimental.pallas import tpu as pltpu
from jax.sharding import PartitionSpec as P

REPULSION = 1.0
KERNEL_SCALE = 0.08
TIME_STEP = 0.2
HIGHEST = lax.Precision.HIGHEST
MESH = pl.DeviceIdType.MESH
F32 = jnp.float32
BF16 = jnp.bfloat16
STRETCH = math.sqrt(2.0 * math.log2(math.e) / KERNEL_SCALE)
FEATURES = 32
UNROLL = 16


def iota(shape, dim):
    return lax.broadcasted_iota(jnp.int32, shape, dim)


def hdot(a, b):
    return jnp.dot(a, b, preferred_element_type=F32, precision=HIGHEST)


def split2(x):
    high = x.astype(BF16)
    return high, (x - high.astype(F32)).astype(BF16)


def split3(x):
    high = x.astype(BF16).astype(F32)
    rest = x - high
    middle = rest.astype(BF16).astype(F32)
    return high, middle, rest - middle


def bdot(a, b):
    return jnp.dot(a, b, preferred_element_type=F32)


def sum_x(q):
    return jnp.concatenate([q[:1], q[:-1] + q[1:], q[-1:]], axis=0)


def diff_x(q):
    return jnp.concatenate([-q[:1], q[:-1] - q[1:], q[-1:]], axis=0)


def body(sizes, stiff_hbm, dens_hbm, load_hbm, alive_hbm, coords_ref, nodes_ref, routes_ref, pairt_ref, pair_ref,
         vout_ref, sout_ref, *scratch):
    (stiff_ref, dens_ref, load_ref, alive_ref, in_sem, mod, big_f, rim_f, load_f, load_r, vel, vel_r, disp, disp_r, minv, minv_r, route_all, pos_all, slots, feat_a, feat_b, take_a, turned_b, give_b,
     partial, send_f, ret, back_pick, choose, pair_hot, rank_in, row_pick, lane_pick, lane_turn, flat, touch, scatter_l,
     x_send, x_recv, y_send, y_recv, edge_send, edge_recv, z_send, z_recv, zx_recv, line_send, line_recv,
     route_ss, route_rs, pos_ss, pos_rs, ret_ss, ret_rs, halo_ss, halo_rs) = scratch
    count_x, count_y, cx, cy, cz, sb, npair, steps, nz, cap = sizes
    nx = cx + 1
    rows = 16
    nslots = nz * cap
    ix, iy, iz = lax.axis_index("gx"), lax.axis_index("gy"), lax.axis_index("gz")
    lanes = iota((rows, cz), 1)
    lane3 = iota((1, 1, cz), 2)

    def roll(v, shift, axis):
        return pltpu.roll(v, shift % v.shape[axis], axis)

    inputs = [pltpu.make_async_copy(a, b, in_sem.at[k]) for k, (a, b) in enumerate((
        (stiff_hbm, stiff_ref), (alive_hbm, alive_ref), (load_hbm, load_ref), (dens_hbm, dens_ref)))]
    for c in inputs:
        c.start()

    for ref in (x_recv, y_send, y_recv, edge_recv, z_recv, zx_recv, line_recv, mod, feat_a, feat_b, send_f):
        ref[...] = jnp.zeros(ref.shape, ref.dtype)

    sides = (("gx", ix, count_x), ("gy", iy, count_y), ("gz", iz, nz))
    ways = sorted((d for d in itertools.product((-1, 0, 1), repeat=3) if any(d)), key=lambda d: (-abs(d[2]), -sum(map(abs, d))))

    def there(d, sign):
        return functools.reduce(jnp.logical_and, [
            (at + sign * step >= 0) & (at + sign * step < count) for step, (_, at, count) in zip(d, sides) if step])

    def neighbor(d):
        return {name: at + step for step, (name, at, _) in zip(d, sides) if step}

    sends = [there(d, 1) for d in ways]
    gets = [there(d, -1) for d in ways]
    barrier = pltpu.get_barrier_semaphore()
    expect = jnp.int32(0)
    for d, here in zip(ways, sends):
        @pl.when(here)
        def _():
            pl.semaphore_signal(barrier, inc=1, device_id=neighbor(d), device_id_type=MESH)
        expect = expect + jnp.where(here, 1, 0)
    for other in (range(1, nz) if nz > 2 else ()):
        far = lax.rem(iz + other, nz)
        apart = jnp.logical_and(far != iz - 1, far != iz + 1)

        @pl.when(apart)
        def _():
            pl.semaphore_signal(barrier, inc=1, device_id={"gz": far}, device_id_type=MESH)
        expect = expect + jnp.where(apart, 1, 0)
    pl.semaphore_wait(barrier, expect)

    def column(send_ref, recv_ref, ss, rs):
        out = []
        for other in range(1, nz):
            to = lax.rem(iz + other, nz)
            out.append(pltpu.make_async_remote_copy(
                src_ref=send_ref(to), dst_ref=recv_ref, send_sem=ss.at[other - 1], recv_sem=rs.at[other - 1],
                device_id={"gz": to}, device_id_type=MESH))
        return out

    def pos_copies(phase):
        return column(lambda to: pos_all.at[phase, iz], pos_all.at[phase, iz], pos_ss.at[phase], pos_rs.at[phase])

    def ret_copies(t):
        return column(lambda to: send_f.at[t, to], ret.at[t, iz], ret_ss.at[t], ret_rs.at[t])

    route_copies = column(lambda to: route_all.at[iz], route_all.at[iz], route_ss, route_rs)

    route_all[iz] = jnp.full((8, 128), -1, jnp.int32)
    route_all[iz, 0:steps, 0:sb] = routes_ref[...]
    for x in range(3):
        pos_all[0, iz, :, x * 128:(x + 1) * 128] = coords_ref[x]
    for c in route_copies + pos_copies(0):
        c.start()

    for c in inputs:
        c.wait()
    for t in range(steps):
        for i in range(cx):
            mod[t, i, 0:cy, :] = stiff_ref[:, i, :] * alive_ref[t, :, i, :].astype(F32)
    for c in range(4):
        for i in range(cx):
            mod[steps + c, i, 0:cy, :] = 0.125 * (load_ref[c, :, i, :] if c < 3 else dens_ref[:, i, :])
    rim = jnp.zeros((rows, cz), F32)
    for c in range(4):
        q = sum_x(mod[steps + c])
        q = q + roll(q, 1, 1)
        r = roll(q, 1, 2)
        load_f[c] = q + jnp.where(lane3 > 0, r, 0.0)
        for i in range(nx):
            at = c * nx + i
            rim = rim + jnp.where(lanes == at, roll(r[i], at, 1), 0.0)
    load_r[...] = rim

    ids = nodes_ref[...]
    row = lax.shift_right_logical(ids, jnp.full(ids.shape, cz.bit_length() - 1, jnp.int32))
    lane = ids & (cz - 1)
    grid_rows = cx * cy
    lane_t = jnp.transpose(jnp.concatenate([lane.astype(F32), jnp.zeros((128 - sb, 128), F32)], axis=0))
    for s in range(sb):
        row_pick[s] = (iota((grid_rows, 128), 0) == row[s:s + 1, :]).astype(F32).astype(BF16)
        hot = (iota((cz, 128), 0) == lane[s:s + 1, :]).astype(F32).astype(BF16)
        lane_pick[s, 0:cz, :] = hot
        lane_pick[s, cz:2 * cz, :] = hot
        col = jnp.broadcast_to(lane_t[:, s:s + 1], (128, cz))
        hot = (iota((128, cz), 1).astype(F32) == col).astype(F32).astype(BF16)
        lane_turn[s * 256:s * 256 + 128, :] = hot
        lane_turn[s * 256 + 128:s * 256 + 256, :] = hot

    def wait_all(copies):
        for c in copies:
            c.wait()

    wait_all(route_copies)
    upper = (iota((128, 128), 0) <= iota((128, 128), 1)).astype(F32)
    own = route_all[iz]
    for b in range(nz):
        hits = (route_all[b] == iz).astype(F32)
        rank_in[b] = jnp.where(hits > 0, jnp.dot(hits, upper, preferred_element_type=F32), 0.0)
    slot8 = nz * 8
    picks = []
    for b in range(nz):
        hits = (own == b).astype(F32)
        picks.append(jnp.where(hits > 0, jnp.dot(hits, upper, preferred_element_type=F32), 0.0))
    ranks8 = (iota((8, 128), 0) + 1).astype(F32)
    live8 = iota((8, 128), 0) < cap
    wide = 4 * npair
    spread4 = (lax.shift_right_logical(iota((npair, wide), 1), jnp.full((npair, wide), 2, jnp.int32))
               == iota((npair, wide), 0)).astype(F32)
    for t in range(steps):
        parts = [jnp.where((picks[b][t:t + 1, :] == ranks8) & live8, 1.0, 0.0) for b in range(nz)]
        table = jnp.concatenate(parts + [jnp.zeros((128 - slot8, 128), F32)], axis=0)
        back_pick[t] = jnp.transpose(table)[0:sb, :]
        hots = [jnp.where(rank_in[b, t:t + 1, :] == ranks8[0:cap], 1.0, 0.0) for b in range(nz)]
        table = jnp.concatenate([roll(hots[b], b * sb, 1) for b in range(nz)], axis=0)
        choose[t] = table
        live = jnp.sum(table, axis=1, keepdims=True)
        pair4 = bdot(pairt_ref[t].astype(F32), spread4)
        slot = iota((nslots, wide), 0).astype(F32)
        is_first = pair4[0:1, :] == slot
        both = (jnp.sum(jnp.where(is_first, live, 0.0), axis=0, keepdims=True)
                * jnp.sum(jnp.where(pair4[1:2, :] == slot, live, 0.0), axis=0, keepdims=True))
        hot = jnp.where(is_first, both, 0.0)
        part = iota((nslots, wide), 1) & 3
        for c in range(4):
            pair_hot[t, c * nslots:(c + 1) * nslots, :] = jnp.where(part == c, hot, 0.0).astype(BF16)

    ones = jnp.ones((nslots, 128), F32)

    def put(ref, at, value):
        ref[pl.ds(at, nslots, stride=FEATURES), :] = value

    for at in (3, 28, 29):
        put(feat_b, at, ones)
    for at in (19, 23, 27):
        put(feat_a, at, ones)

    def gather(phase):
        for c in range(3):
            for i in range(cx):
                flat[c * grid_rows + i * cy:c * grid_rows + (i + 1) * cy, :] = disp[c, i, 0:cy, :]
        high, low = split2(flat[...])
        left = jnp.concatenate([high, low], axis=1)
        for s in range(0, sb, 2):
            got = bdot(left, jnp.concatenate([lane_pick[s], lane_pick[s + 1]], axis=1))
            for h in range(2):
                mask = iota((grid_rows, 128), 0) == row[s + h:s + h + 1, :]
                for c in range(3):
                    part = jnp.where(mask, got[c * grid_rows:(c + 1) * grid_rows, h * 128:(h + 1) * 128], 0.0)
                    pos_all[phase, iz, s + h:s + h + 1, c * 128:(c + 1) * 128] = (
                        jnp.sum(part, axis=0, keepdims=True) + coords_ref[c, s + h:s + h + 1, :])

    def build_slots(t, phase):
        parts = split3(STRETCH * pos_all[phase].reshape(nz * sb, 384))
        got = bdot(choose[t, :, 0:nz * sb].astype(BF16), jnp.concatenate([p.astype(BF16) for p in parts], axis=1))
        norm = jnp.zeros((nslots, 128), F32)
        for c in range(3):
            high, middle, low = (got[:, k * 384 + c * 128:k * 384 + (c + 1) * 128] for k in range(3))
            x = high + middle + low
            slots[c] = x
            norm = norm - 0.5 * (x * x)
            for at in (0, 16, 20):
                put(feat_b, at + c, high)
            for at in (4, 24):
                put(feat_b, at + c, middle)
            put(feat_b, 8 + c, low)
            for at in (0, 8, 24):
                put(feat_a, at + c, high)
            for at in (4, 16):
                put(feat_a, at + c, middle)
            put(feat_a, 20 + c, low)
        for value, at_b, at_a in zip(split3(norm), (27, 23, 19), (3, 28, 29)):
            put(feat_b, at_b, value)
            put(feat_a, at_a, value)
        for k in range(nslots):
            at = k * FEATURES
            tile = feat_a[at:at + FEATURES, :].astype(BF16)
            take_a[k] = jnp.concatenate([tile] * 4, axis=0)
            give_b[k] = feat_b[at:at + 16, :].astype(BF16)
        for g in range(nslots // 4):
            turned = jnp.transpose(feat_b[g * 128:(g + 1) * 128, :])
            for k in range(4):
                mine = (iota((128, 128), 1) >= k * FEATURES) & (iota((128, 128), 1) < (k + 1) * FEATURES)
                turned_b[4 * g + k] = jnp.where(mine, turned, 0.0).astype(BF16)

    upper_half = iota((8, 128), 0) < 4

    def pair_range(t, start, stop):
        def one(q):
            p = pair_ref[t, 0, q]
            r = pair_ref[t, 1, q]
            w = jnp.exp2(bdot(turned_b[r], take_a[p]))
            high, low = split2(w)
            give = give_b[r]
            out = bdot(jnp.concatenate([give, give], axis=1), jnp.concatenate([high, low], axis=0))
            out = out[0:8] + out[8:16]
            return out + roll(out, 4, 0)

        def some(at, carry):
            for u in range(0, UNROLL, 2):
                q = start + at * UNROLL + u
                two = jnp.where(upper_half, one(q), one(q + 1))
                partial[pl.ds(pl.multiple_of(q * 4, 8), 8), :] = two
            return carry

        lax.fori_loop(0, (stop - start) // UNROLL, some, 0)

    def finish_pairs(t):
        total = jnp.zeros((4 * nslots, 128), F32)
        for piece in split3(partial[...]):
            total = total + bdot(pair_hot[t], piece.astype(BF16))
        weight = total[3 * nslots:4 * nslots]
        for c in range(3):
            force = (slots[c] * weight - total[c * nslots:(c + 1) * nslots]) * (REPULSION / STRETCH)
            for b in range(nz):
                send_f[t, b, 0:cap, c * 128:(c + 1) * 128] = force[b * cap:(b + 1) * cap]
        for c in ret_copies(t):
            c.start()
        ret[t, iz] = send_f[t, iz]

    def scatter(t):
        wait_all(ret_copies(t))
        halves = split2(ret[t].reshape(slot8, 384))
        force = bdot(back_pick[t, :, 0:slot8].astype(BF16), jnp.concatenate(halves, axis=1))
        for c in range(3):
            for s in range(sb):
                for h in range(2):
                    at = h * 384 + c * 128
                    line = jnp.broadcast_to(force[s:s + 1, at:at + 128], (16, 128)).astype(BF16)
                    spread = row_pick[s].reshape(grid_rows // 16, 16, 128) * line[None]
                    scatter_l[2 * s + h, c * grid_rows:(c + 1) * grid_rows, :] = spread.reshape(grid_rows, 128)
        left = jnp.concatenate([scatter_l[k] for k in range(2 * sb)], axis=1)
        touch[...] = bdot(left, lane_turn[...])

    def corners(field, rim_value, c):
        u = field[c]
        edge = jnp.stack([roll(rim_value, -(c * nx + i), 1) for i in range(nx)])
        above = roll(jnp.where(lane3 == 0, edge, u), -1, 2)
        both = u + above
        step = above - u
        shifted = roll(both, -1, 1)
        return both + shifted, shifted - both, step + roll(step, -1, 1)

    def stress_of(modulus):
        grads = []
        rim_value = disp_r[...]
        for c in range(3):
            mean, along_y, along_z = corners(disp, rim_value, c)
            grads.append((0.25 * (mean[1:] - mean[:-1]), 0.25 * (along_y[1:] + along_y[:-1]),
                          0.25 * (along_z[1:] + along_z[:-1])))
        trace = grads[0][0] + grads[1][1] + grads[2][2]
        return (modulus * (2.0 * grads[0][0] + trace), modulus * (2.0 * grads[1][1] + trace),
                modulus * (2.0 * grads[2][2] + trace), modulus * (grads[0][1] + grads[1][0]),
                modulus * (grads[1][2] + grads[2][1]), modulus * (grads[0][2] + grads[2][0]))

    def internal(t):
        s = stress_of(mod[t])
        table = ((s[0], s[3], s[5]), (s[3], s[1], s[4]), (s[5], s[4], s[2]))
        rim = load_r[...]
        for c in range(3):
            a0 = -0.25 * diff_x(table[c][0])
            ay = -0.25 * sum_x(table[c][1])
            az = -0.25 * sum_x(table[c][2])
            a = (a0 - ay) + roll(a0 + ay, 1, 1)
            b = az + roll(az, 1, 1)
            r = roll(a + b, 1, 2)
            big_f[c] = load_f[c] + (a - b) + jnp.where(lane3 > 0, r, 0.0)
            for i in range(nx):
                at = c * nx + i
                rim = rim + jnp.where(lanes == at, roll(r[i], at, 1), 0.0)
        rim_f[...] = rim

    line_lanes = iota((1, cz), 1)
    row_at = iota((rows, cz), 0)

    def halo_copies(t, comps, used):
        out = []
        for n, d in enumerate(ways):
            wx, wy, wz = (0 if step < 0 else 1 for step in d)
            dx, dy, dz = d
            if dz and dy:
                pair = line_send.at[t, wz, wy], line_recv.at[t, wz, wy, dx + 1]
            elif dz and dx:
                pair = z_send.at[t, wz], zx_recv.at[t, wz, wx]
            elif dz:
                pair = z_send.at[t, wz], z_recv.at[t, wz]
            elif dx and dy:
                pair = edge_send.at[t, wx, wy], edge_recv.at[t, wx, wy]
            elif dx:
                pair = x_send.at[t, wx, 0:comps + 1], x_recv.at[t, wx, 0:comps + 1]
            else:
                pair = y_send.at[t, wy, 0:used], y_recv.at[t, wy, 0:used]
            out.append(pltpu.make_async_remote_copy(
                src_ref=pair[0], dst_ref=pair[1], send_sem=halo_ss.at[t, n], recv_sem=halo_rs.at[t, n],
                device_id=neighbor(d), device_id_type=MESH))
        return out

    def halo(t, filler):
        comps = 4 if t == 0 else 3
        used = -(-(1 + comps * nx) // 8) * 8
        lines = ((0, 0), (1, cy))
        packed = jnp.zeros((rows, cz), F32)
        for c in range(comps):
            for i in range(nx):
                at = c * nx + i
                packed = jnp.where(lanes == at, roll(big_f[c, i], at, 1), packed)
        z_send[t, 0] = packed
        z_send[t, 1] = rim_f[...]
        for wy, line in lines:
            line_send[t, 0, wy] = packed[line:line + 1]
            line_send[t, 1, wy] = rim_f[line:line + 1]
        for wx, plane in ((0, 0), (1, cx)):
            x_send[t, wx, 0] = rim_f[...]
            for c in range(comps):
                x_send[t, wx, 1 + c] = big_f[c, plane]
            for wy, line in lines:
                edge_send[t, wx, wy, 0:1] = rim_f[line:line + 1]
                for c in range(comps):
                    edge_send[t, wx, wy, 1 + c:2 + c] = big_f[c, plane, line:line + 1]
        for wy, line in lines:
            y_send[t, wy, 0:1] = rim_f[line:line + 1]
            for c in range(comps):
                for i in range(nx):
                    at = 1 + c * nx + i
                    y_send[t, wy, at:at + 1] = big_f[c, i, line:line + 1]
        copies = halo_copies(t, comps, used)
        for copy, here in zip(copies, sends):
            @pl.when(here)
            def _():
                copy.start()

        filler()
        for copy, here, back in zip(copies, sends, gets):
            @pl.when(here)
            def _():
                copy.wait_send()

            @pl.when(back)
            def _():
                copy.wait_recv()

        def across(tile, wx):
            at = line_lanes if tile.shape[0] == 1 else lanes
            mine = functools.reduce(jnp.logical_or, [at == c * nx + (0 if wx else cx) for c in range(comps)])
            return jnp.where(mine, roll(tile, -cx if wx else cx, 1), 0.0)

        def fold(base, faces, edges, corners_):
            for wx in range(2):
                base = base + across(faces[wx], wx)
            for wy, line in ((1, 0), (0, cy)):
                value = edges[wy] + across(corners_[0][wy], 0) + across(corners_[1][wy], 1)
                base = base + jnp.where(row_at == line, value, 0.0)
            return base

        folded = [fold(z_recv[t, w], [zx_recv[t, w, wx] for wx in range(2)], [line_recv[t, w, wy, 1] for wy in range(2)],
                       [[line_recv[t, w, wy, 2 * wx] for wy in range(2)] for wx in range(2)]) for w in range(2)]
        rim_f[...] = folded[0] + fold(
            rim_f[...], [x_recv[t, wx, 0] for wx in range(2)], [y_recv[t, wy, 0:1] for wy in range(2)],
            [[edge_recv[t, wx, wy, 0:1] for wy in range(2)] for wx in range(2)])
        for c in range(comps):
            big_f[c, 0] = big_f[c, 0] + x_recv[t, 1, 1 + c]
            big_f[c, cx] = big_f[c, cx] + x_recv[t, 0, 1 + c]
        for wy, line in ((1, 0), (0, cy)):
            for c in range(comps):
                for i in range(nx):
                    at = 1 + c * nx + i
                    add = y_recv[t, wy, at:at + 1]
                    if i in (0, cx):
                        wx = 1 if i == 0 else 0
                        add = add + edge_recv[t, wx, wy, 1 + c:2 + c]
                    big_f[c, i, line:line + 1] = big_f[c, i, line:line + 1] + add
        for c in range(comps):
            for i in range(nx):
                at = c * nx + i
                big_f[c, i] = big_f[c, i] + jnp.where(lanes == 0, roll(folded[1], -at, 1), 0.0)

    early = npair // 4 // UNROLL * UNROLL

    def contact(t, phase):
        if phase > 0:
            wait_all(pos_copies(phase))
            build_slots(t, phase)
            pair_range(t, 0, npair)
        else:
            pair_range(t, early, npair)
        finish_pairs(t)

    wait_all(pos_copies(0))
    build_slots(0, 0)
    pair_range(0, 0, npair)
    finish_pairs(0)
    build_slots(1, 0)
    pair_range(1, 0, early)

    for t in range(steps):
        if t == 0:
            big_f[...] = load_f[...]
            rim_f[...] = load_r[...]
        else:
            if t + 1 < steps:
                gather(t)
                for c in pos_copies(t):
                    c.start()
            internal(t)
        scatter(t)
        for c in range(3):
            for i in range(cx):
                at = c * grid_rows + i * cy
                big_f[c, i, 0:cy, :] = big_f[c, i, 0:cy, :] + touch[at:at + cy, :]
        halo(t, functools.partial(contact, t + 1, t) if t + 1 < steps else lambda: None)
        if t == 0:
            mass = big_f[3]
            minv[...] = jnp.where(mass > 0.0, 1.0 / mass, 0.0)
            held = jnp.where((lanes >= 3 * nx) & (lanes < 4 * nx), rim_f[...], 0.0)
            spread = roll(held, -3 * nx, 1) + roll(held, -2 * nx, 1) + roll(held, -nx, 1)
            minv_r[...] = jnp.where(spread > 0.0, 1.0 / spread, 0.0)
            for c in range(3):
                vel[c] = TIME_STEP * (big_f[c] * minv[...])
            vel_r[...] = TIME_STEP * (rim_f[...] * minv_r[...])
            disp[...] = TIME_STEP * vel[...]
            disp_r[...] = TIME_STEP * vel_r[...]
        else:
            for c in range(3):
                vel[c] = vel[c] + TIME_STEP * (big_f[c] * minv[...])
            vel_r[...] = vel_r[...] + TIME_STEP * (rim_f[...] * minv_r[...])
            disp[...] = disp[...] + TIME_STEP * vel[...]
            disp_r[...] = disp_r[...] + TIME_STEP * vel_r[...]

    rim_value = vel_r[...]
    for c in range(3):
        mean, _, _ = corners(vel, rim_value, c)
        mean = 0.125 * (mean[1:] + mean[:-1])
        for i in range(cx):
            vout_ref[c, :, i, :] = mean[i, 0:cy, :]
    s = stress_of(mod[steps - 1])
    for c in range(6):
        for i in range(cx):
            sout_ref[c, :, i, :] = s[c][i, 0:cy, :]


def per_device(stiffness, density, load, alive, surf_coords, surf_nodes, routes, pairs):
    cx, cy, cz = stiffness.shape
    steps = alive.shape[0]
    sb = surf_coords.shape[0]
    npair = pairs.shape[2]
    count_x, count_y, nz = (lax.axis_size(a) for a in ("gx", "gy", "gz"))
    cap = max(sb // 4, sb // nz)
    nx = cx + 1
    pairt = jnp.transpose(pairs[:, 0], (0, 2, 1))
    sizes = (count_x, count_y, cx, cy, cz, sb, npair, steps, nz, cap)
    nslots = nz * cap
    vm = lambda *shape: pltpu.VMEM(shape, F32)
    vh = lambda *shape: pltpu.VMEM(shape, BF16)
    dma = lambda *shape: pltpu.SemaphoreType.DMA(shape)
    column = max(nz - 1, 1)
    scratch = [
        vm(cy, cx, cz), vm(cy, cx, cz), vm(3, cy, cx, cz), pltpu.VMEM((steps, cy, cx, cz), jnp.int32), dma(4),
        vm(steps + 4, cx, 16, cz), vm(4, nx, 16, cz), vm(16, cz), vm(4, nx, 16, cz), vm(16, cz),
        vm(3, nx, 16, cz), vm(16, cz), vm(3, nx, 16, cz), vm(16, cz), vm(nx, 16, cz), vm(16, cz),
        pltpu.VMEM((nz, 8, 128), jnp.int32), vm(steps - 1, nz, sb, 384), vm(3, nslots, 128),
        vm(nslots * FEATURES, 128), vm(nslots * FEATURES, 128), vh(nslots, 128, 128), vh(nslots, 128, 128), vh(nslots, 16, 128),
        vm(4 * npair, 128), vm(steps, nz, 8, 384), vm(steps, nz, 8, 384), vm(steps, sb, 128), vm(steps, nslots, 128), vh(steps, 4 * nslots, 4 * npair), vm(nz, 8, 128),
        vh(sb, cx * cy, 128), vh(sb, 2 * cz, 128), vh(2 * sb * 128, cz), vm(3 * cx * cy, cz), vm(3 * cx * cy, cz),
        vh(2 * sb, 3 * cx * cy, 128),
        vm(steps, 2, 5, 16, cz), vm(steps, 2, 5, 16, cz), vm(steps, 2, 40, cz), vm(steps, 2, 40, cz),
        vm(steps, 2, 2, 8, cz), vm(steps, 2, 2, 8, cz),
        vm(steps, 2, 16, cz), vm(steps, 2, 16, cz), vm(steps, 2, 2, 16, cz), vm(steps, 2, 2, 1, cz), vm(steps, 2, 2, 3, 1, cz),
        dma(column), dma(column), dma(steps - 1, column), dma(steps - 1, column), dma(steps, column), dma(steps, column),
        dma(steps, 26), dma(steps, 26),
    ]
    vmem = pl.BlockSpec(memory_space=pltpu.VMEM)
    vel, stress = pl.pallas_call(
        functools.partial(body, sizes),
        out_shape=(jax.ShapeDtypeStruct((3, cy, cx, cz), F32), jax.ShapeDtypeStruct((6, cy, cx, cz), F32)),
        in_specs=[pl.BlockSpec(memory_space=pltpu.MemorySpace.HBM)] * 4 + [vmem] * 4 + [pl.BlockSpec(memory_space=pltpu.SMEM)],
        out_specs=(vmem, vmem),
        scratch_shapes=scratch,
        compiler_params=pltpu.CompilerParams(collective_id=0, has_side_effects=True, vmem_limit_bytes=56 * 1024 * 1024),
    )(jnp.swapaxes(stiffness, 0, 1), jnp.swapaxes(density, 0, 1), jnp.swapaxes(load, 1, 2), jnp.swapaxes(alive, 1, 2),
      jnp.swapaxes(surf_coords, 0, 1), surf_nodes, routes, pairt, pairt)
    return jnp.swapaxes(vel, 1, 2), jnp.swapaxes(stress, 1, 2)


def solution(mesh):
    return jax.shard_map(
        per_device,
        mesh=mesh,
        in_specs=(
            P("gx", "gy", "gz"),
            P("gx", "gy", "gz"),
            P(None, "gx", "gy", "gz"),
            P(None, "gx", "gy", "gz"),
            P(("gx", "gy", "gz"), None, None),
            P(("gx", "gy", "gz"), None),
            P(None, ("gx", "gy", "gz")),
            P(None, ("gx", "gy", "gz"), None, None),
        ),
        out_specs=(P(None, "gx", "gy", "gz"), P(None, "gx", "gy", "gz")),
        check_vma=False,
    )
```

```python
import functools
import itertools
import math

import jax
import jax.numpy as jnp
from jax import lax
from jax.experimental import pallas as pl
from jax.experimental.pallas import tpu as pltpu
from jax.sharding import PartitionSpec as P

REPULSION = 1.0
KERNEL_SCALE = 0.08
TIME_STEP = 0.2
HIGHEST = lax.Precision.HIGHEST
MESH = pl.DeviceIdType.MESH
F32 = jnp.float32
BF16 = jnp.bfloat16
STRETCH = math.sqrt(2.0 * math.log2(math.e) / KERNEL_SCALE)
FEATURES = 32
UNROLL = 32


def iota(shape, dim):
    return lax.broadcasted_iota(jnp.int32, shape, dim)


def hdot(a, b):
    return jnp.dot(a, b, preferred_element_type=F32, precision=HIGHEST)


def split2(x):
    high = x.astype(BF16)
    return high, (x - high.astype(F32)).astype(BF16)


def split3(x):
    high = x.astype(BF16).astype(F32)
    rest = x - high
    middle = rest.astype(BF16).astype(F32)
    return high, middle, rest - middle


def bdot(a, b):
    return jnp.dot(a, b, preferred_element_type=F32)


def sum_x(q):
    return jnp.concatenate([q[:1], q[:-1] + q[1:], q[-1:]], axis=0)


def diff_x(q):
    return jnp.concatenate([-q[:1], q[:-1] - q[1:], q[-1:]], axis=0)


def body(sizes, stiff_hbm, dens_hbm, load_hbm, alive_hbm, coords_ref, nodes_ref, routes_ref, pairt_ref, pair_ref,
         vout_ref, sout_ref, *scratch):
    (stiff_ref, dens_ref, load_ref, alive_ref, in_sem, mod, big_f, rim_f, load_f, load_r, vel, vel_r, disp, disp_r, minv, minv_r, route_all, pos_all, slots, parts, take_a, turned_b, give_b,
     partial, send_f, ret, back_pick, choose, pair_hot, rank_in, row_pick, lane_pick, lane_turn, flat, touch, scatter_l,
     x_send, x_recv, y_send, y_recv, edge_send, edge_recv, z_send, z_recv, zx_recv, line_send, line_recv,
     route_ss, route_rs, pos_ss, pos_rs, ret_ss, ret_rs, halo_ss, halo_rs) = scratch
    count_x, count_y, cx, cy, cz, sb, npair, steps, nz, cap = sizes
    nx = cx + 1
    rows = 16
    nslots = nz * cap
    ix, iy, iz = lax.axis_index("gx"), lax.axis_index("gy"), lax.axis_index("gz")
    lanes = iota((rows, cz), 1)
    lane3 = iota((1, 1, cz), 2)

    def roll(v, shift, axis):
        return pltpu.roll(v, shift % v.shape[axis], axis)

    inputs = [pltpu.make_async_copy(a, b, in_sem.at[k]) for k, (a, b) in enumerate((
        (stiff_hbm, stiff_ref), (alive_hbm, alive_ref), (load_hbm, load_ref), (dens_hbm, dens_ref)))]
    for c in inputs:
        c.start()

    def clear(*refs):
        for ref in refs:
            ref[...] = jnp.zeros(ref.shape, ref.dtype)

    clear(x_recv, y_recv, edge_recv, z_recv, zx_recv, line_recv)

    sides = (("gx", ix, count_x), ("gy", iy, count_y), ("gz", iz, nz))
    only_z = nz == 2
    ways = sorted((d for d in itertools.product((-1, 0, 1), repeat=3) if any(d) and not (only_z and d[2] < 0)), key=lambda d: (-abs(d[2]), -sum(map(abs, d))))

    def there(d, sign):
        return functools.reduce(jnp.logical_and, [
            (at + sign * step >= 0) & (at + sign * step < count)
            for step, (name, at, count) in zip(d, sides) if step and not (only_z and name == "gz")] or [jnp.bool_(True)])

    def neighbor(d):
        return {name: 1 - at if only_z and name == "gz" else at + step for step, (name, at, _) in zip(d, sides) if step}

    sends = [there(d, 1) for d in ways]
    gets = [there(d, -1) for d in ways]
    barrier = pltpu.get_barrier_semaphore()
    expect = jnp.int32(0)
    for d, here in zip(ways, sends):
        @pl.when(here)
        def _():
            pl.semaphore_signal(barrier, inc=1, device_id=neighbor(d), device_id_type=MESH)
        expect = expect + jnp.where(here, 1, 0)
    for other in (range(1, nz) if nz > 2 else ()):
        far = lax.rem(iz + other, nz)
        apart = jnp.logical_and(far != iz - 1, far != iz + 1)

        @pl.when(apart)
        def _():
            pl.semaphore_signal(barrier, inc=1, device_id={"gz": far}, device_id_type=MESH)
        expect = expect + jnp.where(apart, 1, 0)
    pl.semaphore_wait(barrier, expect)

    def column(send_ref, recv_ref, ss, rs):
        out = []
        for other in range(1, nz):
            to = lax.rem(iz + other, nz)
            out.append(pltpu.make_async_remote_copy(
                src_ref=send_ref(to), dst_ref=recv_ref, send_sem=ss.at[other - 1], recv_sem=rs.at[other - 1],
                device_id={"gz": to}, device_id_type=MESH))
        return out

    def pos_copies(phase):
        return column(lambda to: pos_all.at[phase, iz], pos_all.at[phase, iz], pos_ss.at[phase], pos_rs.at[phase])

    def ret_copies(t):
        return column(lambda to: send_f.at[t, to], ret.at[t, iz], ret_ss.at[t], ret_rs.at[t])

    route_copies = column(lambda to: route_all.at[iz], route_all.at[iz], route_ss, route_rs)

    route_all[iz] = jnp.full((8, 128), -1, jnp.int32)
    route_all[iz, 0:steps, 0:sb] = routes_ref[...]
    for x in range(3):
        pos_all[0, iz, :, x * 128:(x + 1) * 128] = coords_ref[x]
    for c in route_copies + pos_copies(0):
        c.start()

    clear(mod, parts, send_f, y_send)
    for c in inputs:
        c.wait()
    for t in range(steps):
        for i in range(cx):
            mod[t, i, 0:cy, :] = stiff_ref[:, i, :] * alive_ref[t, :, i, :].astype(F32)
    for c in range(4):
        for i in range(cx):
            mod[steps + c, i, 0:cy, :] = 0.125 * (load_ref[c, :, i, :] if c < 3 else dens_ref[:, i, :])
    rim = jnp.zeros((rows, cz), F32)
    for c in range(4):
        q = sum_x(mod[steps + c])
        q = q + roll(q, 1, 1)
        r = roll(q, 1, 2)
        load_f[c] = q + jnp.where(lane3 > 0, r, 0.0)
        for i in range(nx):
            at = c * nx + i
            rim = rim + jnp.where(lanes == at, roll(r[i], at, 1), 0.0)
    load_r[...] = rim

    ids = nodes_ref[...]
    row = lax.shift_right_logical(ids, jnp.full(ids.shape, cz.bit_length() - 1, jnp.int32))
    lane = ids & (cz - 1)
    grid_rows = cx * cy
    half_rows = grid_rows // 2
    row2 = lax.shift_right_logical(row, jnp.ones(row.shape, jnp.int32))
    lane2 = lane + (row & 1) * cz
    lane_t = jnp.transpose(jnp.concatenate([lane2.astype(F32), jnp.zeros((128 - sb, 128), F32)], axis=0))
    for s in range(sb):
        row_pick[s] = (iota((half_rows, 128), 0) == row2[s:s + 1, :]).astype(F32).astype(BF16)
        hot = (iota((cz, 128), 0) == lane[s:s + 1, :]).astype(F32).astype(BF16)
        lane_pick[s, 0:cz, :] = hot
        lane_pick[s, cz:2 * cz, :] = hot
        col = jnp.broadcast_to(lane_t[:, s:s + 1], (128, 2 * cz))
        lane_turn[s * 128:(s + 1) * 128, :] = (iota((128, 2 * cz), 1).astype(F32) == col).astype(F32).astype(BF16)

    def wait_all(copies):
        for c in copies:
            c.wait()

    wait_all(route_copies)
    upper = (iota((128, 128), 0) <= iota((128, 128), 1)).astype(F32)
    own = route_all[iz]
    for b in range(nz):
        hits = (route_all[b] == iz).astype(F32)
        rank_in[b] = jnp.where(hits > 0, jnp.dot(hits, upper, preferred_element_type=F32), 0.0)
    slot8 = nz * 8
    picks = []
    for b in range(nz):
        hits = (own == b).astype(F32)
        picks.append(jnp.where(hits > 0, jnp.dot(hits, upper, preferred_element_type=F32), 0.0))
    ranks8 = (iota((8, 128), 0) + 1).astype(F32)
    live8 = iota((8, 128), 0) < cap
    wide = 4 * npair
    spread4 = (lax.shift_right_logical(iota((npair, wide), 1), jnp.full((npair, wide), 2, jnp.int32))
               == iota((npair, wide), 0)).astype(F32)
    for t in range(steps):
        rows_ = [jnp.where((picks[b][t:t + 1, :] == ranks8) & live8, 1.0, 0.0) for b in range(nz)]
        table = jnp.concatenate(rows_ + [jnp.zeros((128 - slot8, 128), F32)], axis=0)
        back_pick[t] = jnp.transpose(table)[0:sb, :]
        hots = [jnp.where(rank_in[b, t:t + 1, :] == ranks8[0:cap], 1.0, 0.0) for b in range(nz)]
        table = jnp.concatenate([roll(hots[b], b * sb, 1) for b in range(nz)], axis=0)
        choose[t] = table
        live = jnp.sum(table, axis=1, keepdims=True)
        pair4 = bdot(pairt_ref[t].astype(F32), spread4)
        slot = iota((nslots, wide), 0).astype(F32)
        is_first = pair4[0:1, :] == slot
        both = (jnp.sum(jnp.where(is_first, live, 0.0), axis=0, keepdims=True)
                * jnp.sum(jnp.where(pair4[1:2, :] == slot, live, 0.0), axis=0, keepdims=True))
        hot = jnp.where(is_first, both, 0.0)
        part = iota((nslots, wide), 1) & 3
        for c in range(4):
            pair_hot[t, c * nslots:(c + 1) * nslots, :] = jnp.where(part == c, hot, 0.0).astype(BF16)

    at8 = iota((8, 128), 0)
    upper_half = at8 < 4
    last = (at8 & 3) == 3
    blank = jnp.zeros((8, 128), F32)

    def put(at, value):
        parts[pl.ds(at, nslots, stride=16), :] = value

    def gather(phase):
        for c in range(3):
            for i in range(cx):
                flat[c * grid_rows + i * cy:c * grid_rows + (i + 1) * cy, :] = disp[c, i, 0:cy, :]
        high, low = split2(flat[...])
        left = jnp.concatenate([high, low], axis=1)
        for s in range(0, sb, 2):
            got = bdot(left, jnp.concatenate([lane_pick[s], lane_pick[s + 1]], axis=1))
            for h in range(2):
                mask = iota((grid_rows, 128), 0) == row[s + h:s + h + 1, :]
                for c in range(3):
                    part = jnp.where(mask, got[c * grid_rows:(c + 1) * grid_rows, h * 128:(h + 1) * 128], 0.0)
                    pos_all[phase, iz, s + h:s + h + 1, c * 128:(c + 1) * 128] = (
                        jnp.sum(part, axis=0, keepdims=True) + coords_ref[c, s + h:s + h + 1, :])

    def build_slots(t, phase):
        pieces = split3(STRETCH * pos_all[phase].reshape(nz * sb, 384))
        got = bdot(choose[t, :, 0:nz * sb].astype(BF16), jnp.concatenate([p.astype(BF16) for p in pieces], axis=1))
        norm = jnp.zeros((nslots, 128), F32)
        for c in range(3):
            high, middle, low = (got[:, k * 384 + c * 128:k * 384 + (c + 1) * 128] for k in range(3))
            x = high + middle + low
            slots[c] = x
            norm = norm - 0.5 * (x * x)
            for k, value in enumerate((high, middle, low)):
                put(4 * k + c, value)
        for k, value in enumerate(split3(norm)):
            put(4 * k + 3, value)
        for k in range(nslots):
            main = parts[k * 16:k * 16 + 8, :]
            rest = parts[k * 16 + 8:k * 16 + 16, :]
            swapped = roll(main, 4, 0)
            ones_b = jnp.where(last, 1.0, main)
            tile_b = [main, jnp.where(upper_half, rest, jnp.where(at8 == 7, 1.0, swapped)), ones_b, blank]
            tile_a = [jnp.where(last, 1.0, jnp.where(upper_half, main, swapped)), jnp.where(at8 == 3, 1.0, main),
                      jnp.where(upper_half, rest, jnp.where(at8 == 7, swapped, main)), blank]
            give = [jnp.where(at8 == 7, 0.0, ones_b), jnp.where(at8 < 3, rest, 0.0)]
            take_a[k] = jnp.concatenate(tile_a, axis=0).astype(BF16)
            give_b[k] = jnp.concatenate(give, axis=0).astype(BF16)
            turned_b[k] = jnp.transpose(jnp.concatenate(tile_b, axis=0)).astype(BF16)


    def pair_range(t, start, stop):
        def weigh(q):
            p = pair_ref[t, 0, q]
            r = pair_ref[t, 1, q]
            return bdot(turned_b[r], take_a[p]), give_b[r]

        def gain(exponent, give):
            high, low = split2(jnp.exp2(exponent))
            out = bdot(jnp.concatenate([give, give], axis=1), jnp.concatenate([high, low], axis=0))
            out = out[0:8] + out[8:16]
            return out + roll(out, 4, 0)

        def some(at, carry):
            first = start + at * UNROLL
            ahead = weigh(first)
            for u in range(0, UNROLL, 2):
                both = []
                for k in (u, u + 1):
                    now, ahead = ahead, weigh(first + k + 1) if k + 1 < UNROLL else None
                    both.append(gain(*now))
                partial[pl.ds(pl.multiple_of((first + u) * 4, 8), 8), :] = jnp.where(upper_half, *both)
            return carry

        lax.fori_loop(0, (stop - start) // UNROLL, some, 0)

    def finish_pairs(t):
        total = jnp.zeros((4 * nslots, 128), F32)
        for piece in split3(partial[...]):
            total = total + bdot(pair_hot[t], piece.astype(BF16))
        weight = total[3 * nslots:4 * nslots]
        for c in range(3):
            force = (slots[c] * weight - total[c * nslots:(c + 1) * nslots]) * (REPULSION / STRETCH)
            for b in range(nz):
                send_f[t, b, 0:cap, c * 128:(c + 1) * 128] = force[b * cap:(b + 1) * cap]
        for c in ret_copies(t):
            c.start()
        ret[t, iz] = send_f[t, iz]

    def scatter(t):
        halves = split2(ret[t].reshape(slot8, 384))
        force = bdot(back_pick[t, :, 0:slot8].astype(BF16), jnp.concatenate(halves, axis=1))
        for s in range(sb):
            for h in range(2):
                for c in range(3):
                    at = h * 384 + c * 128
                    line = jnp.broadcast_to(force[s:s + 1, at:at + 128], (16, 128)).astype(BF16)
                    spread = row_pick[s].reshape(half_rows // 16, 16, 128) * line[None]
                    at = (3 * h + c) * half_rows
                    scatter_l[s, at:at + half_rows, :] = spread.reshape(half_rows, 128)
        left = jnp.concatenate([scatter_l[s] for s in range(sb)], axis=1)
        total = bdot(left, lane_turn[...])
        total = total[0:3 * half_rows] + total[3 * half_rows:]
        for odd in range(2):
            touch[pl.ds(odd, 3 * half_rows, stride=2), :] = total[:, odd * cz:(odd + 1) * cz]

    def corners(field, rim_value, c):
        u = field[c]
        edge = jnp.stack([roll(rim_value, -(c * nx + i), 1) for i in range(nx)])
        above = roll(jnp.where(lane3 == 0, edge, u), -1, 2)
        both = u + above
        step = above - u
        shifted = roll(both, -1, 1)
        return both + shifted, shifted - both, step + roll(step, -1, 1)

    def stress_of(modulus):
        grads = []
        rim_value = disp_r[...]
        for c in range(3):
            mean, along_y, along_z = corners(disp, rim_value, c)
            grads.append((0.25 * (mean[1:] - mean[:-1]), 0.25 * (along_y[1:] + along_y[:-1]),
                          0.25 * (along_z[1:] + along_z[:-1])))
        trace = grads[0][0] + grads[1][1] + grads[2][2]
        return (modulus * (2.0 * grads[0][0] + trace), modulus * (2.0 * grads[1][1] + trace),
                modulus * (2.0 * grads[2][2] + trace), modulus * (grads[0][1] + grads[1][0]),
                modulus * (grads[1][2] + grads[2][1]), modulus * (grads[0][2] + grads[2][0]))

    def internal(t):
        s = stress_of(mod[t])
        table = ((s[0], s[3], s[5]), (s[3], s[1], s[4]), (s[5], s[4], s[2]))
        rim = load_r[...]
        for c in range(3):
            a0 = -0.25 * diff_x(table[c][0])
            ay = -0.25 * sum_x(table[c][1])
            az = -0.25 * sum_x(table[c][2])
            a = (a0 - ay) + roll(a0 + ay, 1, 1)
            b = az + roll(az, 1, 1)
            r = roll(a + b, 1, 2)
            big_f[c] = load_f[c] + (a - b) + jnp.where(lane3 > 0, r, 0.0)
            for i in range(nx):
                at = c * nx + i
                rim = rim + jnp.where(lanes == at, roll(r[i], at, 1), 0.0)
        rim_f[...] = rim

    line_lanes = iota((1, cz), 1)
    row_at = iota((rows, cz), 0)

    def halo_copies(t, comps, used):
        out = []
        for n, d in enumerate(ways):
            wx, wy, wz = (0 if step < 0 else 1 for step in d)
            dx, dy, dz = d
            if only_z:
                wz = 1 - iz
            if dz and dy:
                pair = line_send.at[t, wz, wy], line_recv.at[t, wz, wy, dx + 1]
            elif dz and dx:
                pair = z_send.at[t, wz], zx_recv.at[t, wz, wx]
            elif dz:
                pair = z_send.at[t, wz], z_recv.at[t, wz]
            elif dx and dy:
                pair = edge_send.at[t, wx, wy], edge_recv.at[t, wx, wy]
            elif dx:
                pair = x_send.at[t, wx, 0:comps + 1], x_recv.at[t, wx, 0:comps + 1]
            else:
                pair = y_send.at[t, wy, 0:used], y_recv.at[t, wy, 0:used]
            out.append(pltpu.make_async_remote_copy(
                src_ref=pair[0], dst_ref=pair[1], send_sem=halo_ss.at[t, n], recv_sem=halo_rs.at[t, n],
                device_id=neighbor(d), device_id_type=MESH))
        return out

    def halo(t, filler):
        comps = 4 if t == 0 else 3
        used = -(-(1 + comps * nx) // 8) * 8
        lines = ((0, 0), (1, cy))
        packed = jnp.zeros((rows, cz), F32)
        for c in range(comps):
            for i in range(nx):
                at = c * nx + i
                packed = jnp.where(lanes == at, roll(big_f[c, i], at, 1), packed)
        z_send[t, 0] = packed
        z_send[t, 1] = rim_f[...]
        for wy, line in lines:
            line_send[t, 0, wy] = packed[line:line + 1]
            line_send[t, 1, wy] = rim_f[line:line + 1]
        for wx, plane in ((0, 0), (1, cx)):
            x_send[t, wx, 0] = rim_f[...]
            for c in range(comps):
                x_send[t, wx, 1 + c] = big_f[c, plane]
            for wy, line in lines:
                edge_send[t, wx, wy, 0:1] = rim_f[line:line + 1]
                for c in range(comps):
                    edge_send[t, wx, wy, 1 + c:2 + c] = big_f[c, plane, line:line + 1]
        for wy, line in lines:
            y_send[t, wy, 0:1] = rim_f[line:line + 1]
            for c in range(comps):
                for i in range(nx):
                    at = 1 + c * nx + i
                    y_send[t, wy, at:at + 1] = big_f[c, i, line:line + 1]
        copies = halo_copies(t, comps, used)
        for copy, here in zip(copies, sends):
            @pl.when(here)
            def _():
                copy.start()

        filler()
        for copy, here, back in zip(copies, sends, gets):
            @pl.when(here)
            def _():
                copy.wait_send()

            @pl.when(back)
            def _():
                copy.wait_recv()

        def across(tile, wx):
            at = line_lanes if tile.shape[0] == 1 else lanes
            mine = functools.reduce(jnp.logical_or, [at == c * nx + (0 if wx else cx) for c in range(comps)])
            return jnp.where(mine, roll(tile, -cx if wx else cx, 1), 0.0)

        def fold(base, faces, edges, corners_):
            for wx in range(2):
                base = base + across(faces[wx], wx)
            for wy, line in ((1, 0), (0, cy)):
                value = edges[wy] + across(corners_[0][wy], 0) + across(corners_[1][wy], 1)
                base = base + jnp.where(row_at == line, value, 0.0)
            return base

        folded = [fold(z_recv[t, w], [zx_recv[t, w, wx] for wx in range(2)], [line_recv[t, w, wy, 1] for wy in range(2)],
                       [[line_recv[t, w, wy, 2 * wx] for wy in range(2)] for wx in range(2)]) for w in range(2)]
        rim_f[...] = folded[0] + fold(
            rim_f[...], [x_recv[t, wx, 0] for wx in range(2)], [y_recv[t, wy, 0:1] for wy in range(2)],
            [[edge_recv[t, wx, wy, 0:1] for wy in range(2)] for wx in range(2)])
        for c in range(comps):
            big_f[c, 0] = big_f[c, 0] + x_recv[t, 1, 1 + c]
            big_f[c, cx] = big_f[c, cx] + x_recv[t, 0, 1 + c]
        for wy, line in ((1, 0), (0, cy)):
            for c in range(comps):
                for i in range(nx):
                    at = 1 + c * nx + i
                    add = y_recv[t, wy, at:at + 1]
                    if i in (0, cx):
                        wx = 1 if i == 0 else 0
                        add = add + edge_recv[t, wx, wy, 1 + c:2 + c]
                    big_f[c, i, line:line + 1] = big_f[c, i, line:line + 1] + add
        for c in range(comps):
            for i in range(nx):
                at = c * nx + i
                big_f[c, i] = big_f[c, i] + jnp.where(lanes == 0, roll(folded[1], -at, 1), 0.0)

    early = npair // 2 // UNROLL * UNROLL

    def contact(t, phase):
        if phase > 0:
            wait_all(pos_copies(phase))
            build_slots(t, phase)
            pair_range(t, 0, npair)
        else:
            pair_range(t, early, npair)
        finish_pairs(t)

    wait_all(pos_copies(0))
    build_slots(0, 0)
    pair_range(0, 0, npair)
    finish_pairs(0)
    build_slots(1, 0)
    pair_range(1, 0, early)

    for t in range(steps):
        if t == 0:
            big_f[...] = load_f[...]
            rim_f[...] = load_r[...]
            wait_all(ret_copies(t))
        else:
            if t + 1 < steps:
                gather(t)
                for c in pos_copies(t):
                    c.start()
            wait_all(ret_copies(t))
            internal(t)
        scatter(t)
        for c in range(3):
            for i in range(cx):
                at = c * grid_rows + i * cy
                big_f[c, i, 0:cy, :] = big_f[c, i, 0:cy, :] + touch[at:at + cy, :]
        halo(t, functools.partial(contact, t + 1, t) if t + 1 < steps else lambda: None)
        if t == 0:
            mass = big_f[3]
            minv[...] = jnp.where(mass > 0.0, 1.0 / mass, 0.0)
            held = jnp.where((lanes >= 3 * nx) & (lanes < 4 * nx), rim_f[...], 0.0)
            spread = roll(held, -3 * nx, 1) + roll(held, -2 * nx, 1) + roll(held, -nx, 1)
            minv_r[...] = jnp.where(spread > 0.0, 1.0 / spread, 0.0)
            for c in range(3):
                vel[c] = TIME_STEP * (big_f[c] * minv[...])
            vel_r[...] = TIME_STEP * (rim_f[...] * minv_r[...])
            disp[...] = TIME_STEP * vel[...]
            disp_r[...] = TIME_STEP * vel_r[...]
        else:
            for c in range(3):
                vel[c] = vel[c] + TIME_STEP * (big_f[c] * minv[...])
            vel_r[...] = vel_r[...] + TIME_STEP * (rim_f[...] * minv_r[...])
            disp[...] = disp[...] + TIME_STEP * vel[...]
            disp_r[...] = disp_r[...] + TIME_STEP * vel_r[...]

    rim_value = vel_r[...]
    for c in range(3):
        mean, _, _ = corners(vel, rim_value, c)
        mean = 0.125 * (mean[1:] + mean[:-1])
        for i in range(cx):
            vout_ref[c, :, i, :] = mean[i, 0:cy, :]
    s = stress_of(mod[steps - 1])
    for c in range(6):
        for i in range(cx):
            sout_ref[c, :, i, :] = s[c][i, 0:cy, :]


def per_device(stiffness, density, load, alive, surf_coords, surf_nodes, routes, pairs):
    cx, cy, cz = stiffness.shape
    steps = alive.shape[0]
    sb = surf_coords.shape[0]
    npair = pairs.shape[2]
    count_x, count_y, nz = (lax.axis_size(a) for a in ("gx", "gy", "gz"))
    cap = max(sb // 4, sb // nz)
    nx = cx + 1
    pairt = jnp.transpose(pairs[:, 0], (0, 2, 1))
    sizes = (count_x, count_y, cx, cy, cz, sb, npair, steps, nz, cap)
    nslots = nz * cap
    vm = lambda *shape: pltpu.VMEM(shape, F32)
    vh = lambda *shape: pltpu.VMEM(shape, BF16)
    dma = lambda *shape: pltpu.SemaphoreType.DMA(shape)
    column = max(nz - 1, 1)
    scratch = [
        vm(cy, cx, cz), vm(cy, cx, cz), vm(3, cy, cx, cz), pltpu.VMEM((steps, cy, cx, cz), jnp.int32), dma(4),
        vm(steps + 4, cx, 16, cz), vm(4, nx, 16, cz), vm(16, cz), vm(4, nx, 16, cz), vm(16, cz),
        vm(3, nx, 16, cz), vm(16, cz), vm(3, nx, 16, cz), vm(16, cz), vm(nx, 16, cz), vm(16, cz),
        pltpu.VMEM((nz, 8, 128), jnp.int32), vm(steps - 1, nz, sb, 384), vm(3, nslots, 128),
        vm(nslots * 16, 128), vh(nslots, FEATURES, 128), vh(nslots, 128, FEATURES), vh(nslots, 16, 128),
        vm(4 * npair, 128), vm(steps, nz, 8, 384), vm(steps, nz, 8, 384), vm(steps, sb, 128), vm(steps, nslots, 128), vh(steps, 4 * nslots, 4 * npair), vm(nz, 8, 128),
        vh(sb, cx * cy // 2, 128), vh(sb, 2 * cz, 128), vh(sb * 128, 2 * cz), vm(3 * cx * cy, cz), vm(3 * cx * cy, cz),
        vh(sb, 3 * cx * cy, 128),
        vm(steps, 2, 5, 16, cz), vm(steps, 2, 5, 16, cz), vm(steps, 2, 40, cz), vm(steps, 2, 40, cz),
        vm(steps, 2, 2, 8, cz), vm(steps, 2, 2, 8, cz),
        vm(steps, 2, 16, cz), vm(steps, 2, 16, cz), vm(steps, 2, 2, 16, cz), vm(steps, 2, 2, 1, cz), vm(steps, 2, 2, 3, 1, cz),
        dma(column), dma(column), dma(steps - 1, column), dma(steps - 1, column), dma(steps, column), dma(steps, column),
        dma(steps, 26), dma(steps, 26),
    ]
    vmem = pl.BlockSpec(memory_space=pltpu.VMEM)
    vel, stress = pl.pallas_call(
        functools.partial(body, sizes),
        out_shape=(jax.ShapeDtypeStruct((3, cy, cx, cz), F32), jax.ShapeDtypeStruct((6, cy, cx, cz), F32)),
        in_specs=[pl.BlockSpec(memory_space=pltpu.MemorySpace.HBM)] * 4 + [vmem] * 4 + [pl.BlockSpec(memory_space=pltpu.SMEM)],
        out_specs=(vmem, vmem),
        scratch_shapes=scratch,
        compiler_params=pltpu.CompilerParams(collective_id=0, has_side_effects=True, vmem_limit_bytes=56 * 1024 * 1024),
    )(jnp.swapaxes(stiffness, 0, 1), jnp.swapaxes(density, 0, 1), jnp.swapaxes(load, 1, 2), jnp.swapaxes(alive, 1, 2),
      jnp.swapaxes(surf_coords, 0, 1), surf_nodes, routes, pairt, pairt)
    return jnp.swapaxes(vel, 1, 2), jnp.swapaxes(stress, 1, 2)


def solution(mesh):
    return jax.shard_map(
        per_device,
        mesh=mesh,
        in_specs=(
            P("gx", "gy", "gz"),
            P("gx", "gy", "gz"),
            P(None, "gx", "gy", "gz"),
            P(None, "gx", "gy", "gz"),
            P(("gx", "gy", "gz"), None, None),
            P(("gx", "gy", "gz"), None),
            P(None, ("gx", "gy", "gz")),
            P(None, ("gx", "gy", "gz"), None, None),
        ),
        out_specs=(P(None, "gx", "gy", "gz"), P(None, "gx", "gy", "gz")),
        check_vma=False,
    )
```

```python
import functools
import itertools
import math

import jax
import jax.numpy as jnp
from jax import lax
from jax.experimental import pallas as pl
from jax.experimental.pallas import tpu as pltpu
from jax.sharding import PartitionSpec as P

REPULSION = 1.0
KERNEL_SCALE = 0.08
TIME_STEP = 0.2
HIGHEST = lax.Precision.HIGHEST
MESH = pl.DeviceIdType.MESH
F32 = jnp.float32
BF16 = jnp.bfloat16
STRETCH = math.sqrt(2.0 * math.log2(math.e) / KERNEL_SCALE)
FEATURES = 32


def iota(shape, dim):
    return lax.broadcasted_iota(jnp.int32, shape, dim)


def hdot(a, b):
    return jnp.dot(a, b, preferred_element_type=F32, precision=HIGHEST)


def split2(x):
    high = x.astype(BF16)
    return high, (x - high.astype(F32)).astype(BF16)


def split3(x):
    high = x.astype(BF16).astype(F32)
    rest = x - high
    middle = rest.astype(BF16).astype(F32)
    return high, middle, rest - middle


def bdot(a, b):
    return jnp.dot(a, b, preferred_element_type=F32)


def sum_x(q):
    return jnp.concatenate([q[:1], q[:-1] + q[1:], q[-1:]], axis=0)


def diff_x(q):
    return jnp.concatenate([-q[:1], q[:-1] - q[1:], q[-1:]], axis=0)


def body(sizes, stiff_hbm, dens_hbm, load_hbm, alive_hbm, coords_ref, nodes_ref, routes_ref, pairt_ref, pair_ref,
         vout_ref, sout_ref, *scratch):
    (stiff_ref, dens_ref, load_ref, alive_ref, in_sem, mod, big_f, rim_f, load_f, load_r, vel, vel_r, disp, disp_r, minv, minv_r, route_all, pos_all, slots, parts, take_a, turned_b, give_b,
     partial, send_f, ret, back_pick, choose, pair_hot, rank_in, row_pick, lane_pick, lane_turn, flat, touch, scatter_l,
     x_send, x_recv, y_send, y_recv, edge_send, edge_recv, z_send, z_recv, zx_recv, line_send, line_recv,
     route_ss, route_rs, pos_ss, pos_rs, ret_ss, ret_rs, halo_ss, halo_rs) = scratch
    count_x, count_y, cx, cy, cz, sb, npair, steps, nz, cap = sizes
    nx = cx + 1
    rows = 16
    nslots = nz * cap
    ix, iy, iz = lax.axis_index("gx"), lax.axis_index("gy"), lax.axis_index("gz")
    lanes = iota((rows, cz), 1)
    lane3 = iota((1, 1, cz), 2)

    def roll(v, shift, axis):
        return pltpu.roll(v, shift % v.shape[axis], axis)

    inputs = [pltpu.make_async_copy(a, b, in_sem.at[k]) for k, (a, b) in enumerate((
        (stiff_hbm, stiff_ref), (alive_hbm, alive_ref), (load_hbm, load_ref), (dens_hbm, dens_ref)))]
    for c in inputs:
        c.start()

    def clear(*refs):
        for ref in refs:
            ref[...] = jnp.zeros(ref.shape, ref.dtype)

    clear(x_recv, y_recv, edge_recv, z_recv, zx_recv, line_recv)

    sides = (("gx", ix, count_x), ("gy", iy, count_y), ("gz", iz, nz))
    only_z = nz == 2
    ways = sorted((d for d in itertools.product((-1, 0, 1), repeat=3) if any(d) and not (only_z and d[2] < 0)), key=lambda d: (-abs(d[2]), -sum(map(abs, d))))

    def there(d, sign):
        return functools.reduce(jnp.logical_and, [
            (at + sign * step >= 0) & (at + sign * step < count)
            for step, (name, at, count) in zip(d, sides) if step and not (only_z and name == "gz")] or [jnp.bool_(True)])

    def neighbor(d):
        return {name: 1 - at if only_z and name == "gz" else at + step for step, (name, at, _) in zip(d, sides) if step}

    sends = [there(d, 1) for d in ways]
    gets = [there(d, -1) for d in ways]
    barrier = pltpu.get_barrier_semaphore()
    expect = jnp.int32(0)
    for d, here in zip(ways, sends):
        @pl.when(here)
        def _():
            pl.semaphore_signal(barrier, inc=1, device_id=neighbor(d), device_id_type=MESH)
        expect = expect + jnp.where(here, 1, 0)
    for other in (range(1, nz) if nz > 2 else ()):
        far = lax.rem(iz + other, nz)
        apart = jnp.logical_and(far != iz - 1, far != iz + 1)

        @pl.when(apart)
        def _():
            pl.semaphore_signal(barrier, inc=1, device_id={"gz": far}, device_id_type=MESH)
        expect = expect + jnp.where(apart, 1, 0)
    pl.semaphore_wait(barrier, expect)

    def column(send_ref, recv_ref, ss, rs):
        out = []
        for other in range(1, nz):
            to = lax.rem(iz + other, nz)
            out.append(pltpu.make_async_remote_copy(
                src_ref=send_ref(to), dst_ref=recv_ref, send_sem=ss.at[other - 1], recv_sem=rs.at[other - 1],
                device_id={"gz": to}, device_id_type=MESH))
        return out

    def pos_copies(phase):
        return column(lambda to: pos_all.at[phase, iz], pos_all.at[phase, iz], pos_ss.at[phase], pos_rs.at[phase])

    def ret_copies(t):
        return column(lambda to: send_f.at[t, to], ret.at[t, iz], ret_ss.at[t], ret_rs.at[t])

    route_copies = column(lambda to: route_all.at[iz], route_all.at[iz], route_ss, route_rs)

    route_all[iz] = jnp.full((8, 128), -1, jnp.int32)
    route_all[iz, 0:steps, 0:sb] = routes_ref[...]
    for x in range(3):
        pos_all[0, iz, :, x * 128:(x + 1) * 128] = coords_ref[x]
    for c in route_copies + pos_copies(0):
        c.start()

    clear(mod, parts, send_f, y_send)
    for c in inputs:
        c.wait()
    for t in range(steps):
        for i in range(cx):
            mod[t, i, 0:cy, :] = stiff_ref[:, i, :] * alive_ref[t, :, i, :].astype(F32)
    for c in range(4):
        for i in range(cx):
            mod[steps + c, i, 0:cy, :] = 0.125 * (load_ref[c, :, i, :] if c < 3 else dens_ref[:, i, :])
    rim = jnp.zeros((rows, cz), F32)
    for c in range(4):
        q = sum_x(mod[steps + c])
        q = q + roll(q, 1, 1)
        r = roll(q, 1, 2)
        load_f[c] = q + jnp.where(lane3 > 0, r, 0.0)
        for i in range(nx):
            at = c * nx + i
            rim = rim + jnp.where(lanes == at, roll(r[i], at, 1), 0.0)
    load_r[...] = rim

    ids = nodes_ref[...]
    row = lax.shift_right_logical(ids, jnp.full(ids.shape, cz.bit_length() - 1, jnp.int32))
    lane = ids & (cz - 1)
    grid_rows = cx * cy
    half_rows = grid_rows // 2
    row2 = lax.shift_right_logical(row, jnp.ones(row.shape, jnp.int32))
    lane2 = lane + (row & 1) * cz
    lane_t = jnp.transpose(jnp.concatenate([lane2.astype(F32), jnp.zeros((128 - sb, 128), F32)], axis=0))
    for s in range(sb):
        row_pick[s] = (iota((half_rows, 128), 0) == row2[s:s + 1, :]).astype(F32).astype(BF16)
        hot = (iota((cz, 128), 0) == lane[s:s + 1, :]).astype(F32).astype(BF16)
        lane_pick[s, 0:cz, :] = hot
        lane_pick[s, cz:2 * cz, :] = hot
        col = jnp.broadcast_to(lane_t[:, s:s + 1], (128, 2 * cz))
        lane_turn[s * 128:(s + 1) * 128, :] = (iota((128, 2 * cz), 1).astype(F32) == col).astype(F32).astype(BF16)

    def wait_all(copies):
        for c in copies:
            c.wait()

    wait_all(route_copies)
    upper = (iota((128, 128), 0) <= iota((128, 128), 1)).astype(F32)
    own = route_all[iz]
    for b in range(nz):
        hits = (route_all[b] == iz).astype(F32)
        rank_in[b] = jnp.where(hits > 0, jnp.dot(hits, upper, preferred_element_type=F32), 0.0)
    slot8 = nz * 8
    picks = []
    for b in range(nz):
        hits = (own == b).astype(F32)
        picks.append(jnp.where(hits > 0, jnp.dot(hits, upper, preferred_element_type=F32), 0.0))
    ranks8 = (iota((8, 128), 0) + 1).astype(F32)
    live8 = iota((8, 128), 0) < cap
    wide = 4 * npair
    spread4 = (lax.shift_right_logical(iota((npair, wide), 1), jnp.full((npair, wide), 2, jnp.int32))
               == iota((npair, wide), 0)).astype(F32)
    for t in range(steps):
        rows_ = [jnp.where((picks[b][t:t + 1, :] == ranks8) & live8, 1.0, 0.0) for b in range(nz)]
        table = jnp.concatenate(rows_ + [jnp.zeros((128 - slot8, 128), F32)], axis=0)
        back_pick[t] = jnp.transpose(table)[0:sb, :]
        hots = [jnp.where(rank_in[b, t:t + 1, :] == ranks8[0:cap], 1.0, 0.0) for b in range(nz)]
        table = jnp.concatenate([roll(hots[b], b * sb, 1) for b in range(nz)], axis=0)
        choose[t] = table
        live = jnp.sum(table, axis=1, keepdims=True)
        pair4 = bdot(pairt_ref[t].astype(F32), spread4)
        slot = iota((nslots, wide), 0).astype(F32)
        is_first = pair4[0:1, :] == slot
        both = (jnp.sum(jnp.where(is_first, live, 0.0), axis=0, keepdims=True)
                * jnp.sum(jnp.where(pair4[1:2, :] == slot, live, 0.0), axis=0, keepdims=True))
        hot = jnp.where(is_first, both, 0.0)
        part = iota((nslots, wide), 1) & 3
        for c in range(4):
            pair_hot[t, c * nslots:(c + 1) * nslots, :] = jnp.where(part == c, hot, 0.0).astype(BF16)

    at8 = iota((8, 128), 0)
    upper_half = at8 < 4
    last = (at8 & 3) == 3
    blank = jnp.zeros((8, 128), F32)

    def put(at, value):
        parts[pl.ds(at, nslots, stride=16), :] = value

    def gather(phase):
        for c in range(3):
            for i in range(cx):
                flat[c * grid_rows + i * cy:c * grid_rows + (i + 1) * cy, :] = disp[c, i, 0:cy, :]
        high, low = split2(flat[...])
        left = jnp.concatenate([high, low], axis=1)
        for s in range(0, sb, 2):
            got = bdot(left, jnp.concatenate([lane_pick[s], lane_pick[s + 1]], axis=1))
            for h in range(2):
                mask = iota((grid_rows, 128), 0) == row[s + h:s + h + 1, :]
                for c in range(3):
                    part = jnp.where(mask, got[c * grid_rows:(c + 1) * grid_rows, h * 128:(h + 1) * 128], 0.0)
                    pos_all[phase, iz, s + h:s + h + 1, c * 128:(c + 1) * 128] = (
                        jnp.sum(part, axis=0, keepdims=True) + coords_ref[c, s + h:s + h + 1, :])

    def build_slots(t, phase):
        pieces = split3(STRETCH * pos_all[phase].reshape(nz * sb, 384))
        got = bdot(choose[t, :, 0:nz * sb].astype(BF16), jnp.concatenate([p.astype(BF16) for p in pieces], axis=1))
        norm = jnp.zeros((nslots, 128), F32)
        for c in range(3):
            high, middle, low = (got[:, k * 384 + c * 128:k * 384 + (c + 1) * 128] for k in range(3))
            x = high + middle + low
            slots[c] = x
            norm = norm - 0.5 * (x * x)
            for k, value in enumerate((high, middle, low)):
                put(4 * k + c, value)
        for k, value in enumerate(split3(norm)):
            put(4 * k + 3, value)
        for k in range(nslots):
            main = parts[k * 16:k * 16 + 8, :]
            rest = parts[k * 16 + 8:k * 16 + 16, :]
            swapped = roll(main, 4, 0)
            ones_b = jnp.where(last, 1.0, main)
            tile_b = [main, jnp.where(upper_half, rest, jnp.where(at8 == 7, 1.0, swapped)), ones_b, blank]
            tile_a = [jnp.where(last, 1.0, jnp.where(upper_half, main, swapped)), jnp.where(at8 == 3, 1.0, main),
                      jnp.where(upper_half, rest, jnp.where(at8 == 7, swapped, main)), blank]
            give = [jnp.where(at8 == 7, 0.0, ones_b), jnp.where(at8 < 3, rest, 0.0)]
            take_a[k] = jnp.concatenate(tile_a, axis=0).astype(BF16)
            give_b[k] = jnp.concatenate(give, axis=0).astype(BF16)
            turned_b[k] = jnp.transpose(jnp.concatenate(tile_b, axis=0)).astype(BF16)


    def pair_range(t, start, stop):
        count = stop - start

        def weigh(q):
            p = pair_ref[t, 0, q]
            r = pair_ref[t, 1, q]
            return bdot(turned_b[r], take_a[p]), give_b[r]

        def gain(exponent, give):
            high, low = split2(jnp.exp2(exponent))
            out = bdot(jnp.concatenate([give, give], axis=1), jnp.concatenate([high, low], axis=0))
            out = out[0:8] + out[8:16]
            return out + roll(out, 4, 0)

        def some(at, carry):
            first = start + at * count
            ahead = weigh(first)
            for u in range(0, count, 2):
                both = []
                for k in (u, u + 1):
                    now, ahead = ahead, weigh(first + k + 1) if k + 1 < count else None
                    both.append(gain(*now))
                partial[pl.ds(pl.multiple_of((first + u) * 4, 8), 8), :] = jnp.where(upper_half, *both)
            return carry

        lax.fori_loop(0, 1 + jnp.minimum(iz, 0), some, 0)

    def finish_pairs(t):
        total = jnp.zeros((4 * nslots, 128), F32)
        for piece in split3(partial[...]):
            total = total + bdot(pair_hot[t], piece.astype(BF16))
        weight = total[3 * nslots:4 * nslots]
        for c in range(3):
            force = (slots[c] * weight - total[c * nslots:(c + 1) * nslots]) * (REPULSION / STRETCH)
            for b in range(nz):
                send_f[t, b, 0:cap, c * 128:(c + 1) * 128] = force[b * cap:(b + 1) * cap]
        for c in ret_copies(t):
            c.start()
        ret[t, iz] = send_f[t, iz]

    def scatter(t):
        halves = split2(ret[t].reshape(slot8, 384))
        force = bdot(back_pick[t, :, 0:slot8].astype(BF16), jnp.concatenate(halves, axis=1))
        for s in range(sb):
            for h in range(2):
                for c in range(3):
                    at = h * 384 + c * 128
                    line = jnp.broadcast_to(force[s:s + 1, at:at + 128], (16, 128)).astype(BF16)
                    spread = row_pick[s].reshape(half_rows // 16, 16, 128) * line[None]
                    at = (3 * h + c) * half_rows
                    scatter_l[s, at:at + half_rows, :] = spread.reshape(half_rows, 128)
        left = jnp.concatenate([scatter_l[s] for s in range(sb)], axis=1)
        total = bdot(left, lane_turn[...])
        total = total[0:3 * half_rows] + total[3 * half_rows:]
        for odd in range(2):
            touch[pl.ds(odd, 3 * half_rows, stride=2), :] = total[:, odd * cz:(odd + 1) * cz]

    def corners(field, rim_value, c):
        u = field[c]
        edge = jnp.stack([roll(rim_value, -(c * nx + i), 1) for i in range(nx)])
        above = roll(jnp.where(lane3 == 0, edge, u), -1, 2)
        both = u + above
        step = above - u
        shifted = roll(both, -1, 1)
        return both + shifted, shifted - both, step + roll(step, -1, 1)

    def stress_of(modulus):
        grads = []
        rim_value = disp_r[...]
        for c in range(3):
            mean, along_y, along_z = corners(disp, rim_value, c)
            grads.append((mean[1:] - mean[:-1], along_y[1:] + along_y[:-1], along_z[1:] + along_z[:-1]))
        trace = grads[0][0] + grads[1][1] + grads[2][2]
        return (modulus * (2.0 * grads[0][0] + trace), modulus * (2.0 * grads[1][1] + trace),
                modulus * (2.0 * grads[2][2] + trace), modulus * (grads[0][1] + grads[1][0]),
                modulus * (grads[1][2] + grads[2][1]), modulus * (grads[0][2] + grads[2][0]))

    def internal(t):
        s = stress_of(-0.0625 * mod[t])
        table = ((s[0], s[3], s[5]), (s[3], s[1], s[4]), (s[5], s[4], s[2]))
        rim = load_r[...]
        for c in range(3):
            a0 = diff_x(table[c][0])
            ay = sum_x(table[c][1])
            az = sum_x(table[c][2])
            a = (a0 - ay) + roll(a0 + ay, 1, 1)
            b = az + roll(az, 1, 1)
            r = roll(a + b, 1, 2)
            big_f[c] = load_f[c] + (a - b) + jnp.where(lane3 > 0, r, 0.0)
            for i in range(nx):
                at = c * nx + i
                rim = rim + jnp.where(lanes == at, roll(r[i], at, 1), 0.0)
        rim_f[...] = rim

    line_lanes = iota((1, cz), 1)
    row_at = iota((rows, cz), 0)

    def halo_copies(t, comps, used):
        out = []
        for n, d in enumerate(ways):
            wx, wy, wz = (0 if step < 0 else 1 for step in d)
            dx, dy, dz = d
            if only_z:
                wz = 1 - iz
            if dz and dy:
                pair = line_send.at[t, wz, wy], line_recv.at[t, wz, wy, dx + 1]
            elif dz and dx:
                pair = z_send.at[t, wz], zx_recv.at[t, wz, wx]
            elif dz:
                pair = z_send.at[t, wz], z_recv.at[t, wz]
            elif dx and dy:
                pair = edge_send.at[t, wx, wy], edge_recv.at[t, wx, wy]
            elif dx:
                pair = x_send.at[t, wx, 0:comps + 1], x_recv.at[t, wx, 0:comps + 1]
            else:
                pair = y_send.at[t, wy, 0:used], y_recv.at[t, wy, 0:used]
            out.append(pltpu.make_async_remote_copy(
                src_ref=pair[0], dst_ref=pair[1], send_sem=halo_ss.at[t, n], recv_sem=halo_rs.at[t, n],
                device_id=neighbor(d), device_id_type=MESH))
        return out

    def halo(t, filler):
        comps = 4 if t == 0 else 3
        used = -(-(1 + comps * nx) // 8) * 8
        lines = ((0, 0), (1, cy))
        packed = jnp.zeros((rows, cz), F32)
        for c in range(comps):
            for i in range(nx):
                at = c * nx + i
                packed = jnp.where(lanes == at, roll(big_f[c, i], at, 1), packed)
        z_send[t, 0] = packed
        z_send[t, 1] = rim_f[...]
        for wy, line in lines:
            line_send[t, 0, wy] = packed[line:line + 1]
            line_send[t, 1, wy] = rim_f[line:line + 1]
        for wx, plane in ((0, 0), (1, cx)):
            x_send[t, wx, 0] = rim_f[...]
            for c in range(comps):
                x_send[t, wx, 1 + c] = big_f[c, plane]
            for wy, line in lines:
                edge_send[t, wx, wy, 0:1] = rim_f[line:line + 1]
                for c in range(comps):
                    edge_send[t, wx, wy, 1 + c:2 + c] = big_f[c, plane, line:line + 1]
        for wy, line in lines:
            y_send[t, wy, 0:1] = rim_f[line:line + 1]
            for c in range(comps):
                for i in range(nx):
                    at = 1 + c * nx + i
                    y_send[t, wy, at:at + 1] = big_f[c, i, line:line + 1]
        copies = halo_copies(t, comps, used)
        for copy, here in zip(copies, sends):
            @pl.when(here)
            def _():
                copy.start()

        filler()
        for copy, here, back in zip(copies, sends, gets):
            @pl.when(here)
            def _():
                copy.wait_send()

            @pl.when(back)
            def _():
                copy.wait_recv()

        def across(tile, wx):
            at = line_lanes if tile.shape[0] == 1 else lanes
            mine = functools.reduce(jnp.logical_or, [at == c * nx + (0 if wx else cx) for c in range(comps)])
            return jnp.where(mine, roll(tile, -cx if wx else cx, 1), 0.0)

        def fold(base, faces, edges, corners_):
            for wx in range(2):
                base = base + across(faces[wx], wx)
            for wy, line in ((1, 0), (0, cy)):
                value = edges[wy] + across(corners_[0][wy], 0) + across(corners_[1][wy], 1)
                base = base + jnp.where(row_at == line, value, 0.0)
            return base

        folded = [fold(z_recv[t, w], [zx_recv[t, w, wx] for wx in range(2)], [line_recv[t, w, wy, 1] for wy in range(2)],
                       [[line_recv[t, w, wy, 2 * wx] for wy in range(2)] for wx in range(2)]) for w in range(2)]
        rim_f[...] = folded[0] + fold(
            rim_f[...], [x_recv[t, wx, 0] for wx in range(2)], [y_recv[t, wy, 0:1] for wy in range(2)],
            [[edge_recv[t, wx, wy, 0:1] for wy in range(2)] for wx in range(2)])
        for c in range(comps):
            big_f[c, 0] = big_f[c, 0] + x_recv[t, 1, 1 + c]
            big_f[c, cx] = big_f[c, cx] + x_recv[t, 0, 1 + c]
        for wy, line in ((1, 0), (0, cy)):
            for c in range(comps):
                for i in range(nx):
                    at = 1 + c * nx + i
                    add = y_recv[t, wy, at:at + 1]
                    if i in (0, cx):
                        wx = 1 if i == 0 else 0
                        add = add + edge_recv[t, wx, wy, 1 + c:2 + c]
                    big_f[c, i, line:line + 1] = big_f[c, i, line:line + 1] + add
        for c in range(comps):
            for i in range(nx):
                at = c * nx + i
                big_f[c, i] = big_f[c, i] + jnp.where(lanes == 0, roll(folded[1], -at, 1), 0.0)

    def contact(t, phase):
        if phase > 0:
            wait_all(pos_copies(phase))
            build_slots(t, phase)
            pair_range(t, 0, npair)
        finish_pairs(t)

    wait_all(pos_copies(0))
    build_slots(0, 0)
    pair_range(0, 0, npair)
    finish_pairs(0)
    build_slots(1, 0)
    pair_range(1, 0, npair)

    for t in range(steps):
        if t == 0:
            big_f[...] = load_f[...]
            rim_f[...] = load_r[...]
            wait_all(ret_copies(t))
        else:
            if t + 1 < steps:
                gather(t)
                for c in pos_copies(t):
                    c.start()
            wait_all(ret_copies(t))
            internal(t)
        scatter(t)
        for c in range(3):
            for i in range(cx):
                at = c * grid_rows + i * cy
                big_f[c, i, 0:cy, :] = big_f[c, i, 0:cy, :] + touch[at:at + cy, :]
        halo(t, functools.partial(contact, t + 1, t) if t + 1 < steps else lambda: None)
        if t == 0:
            mass = big_f[3]
            minv[...] = jnp.where(mass > 0.0, 1.0 / mass, 0.0)
            held = jnp.where((lanes >= 3 * nx) & (lanes < 4 * nx), rim_f[...], 0.0)
            spread = roll(held, -3 * nx, 1) + roll(held, -2 * nx, 1) + roll(held, -nx, 1)
            minv_r[...] = jnp.where(spread > 0.0, 1.0 / spread, 0.0)
            for c in range(3):
                vel[c] = TIME_STEP * (big_f[c] * minv[...])
            vel_r[...] = TIME_STEP * (rim_f[...] * minv_r[...])
            disp[...] = TIME_STEP * vel[...]
            disp_r[...] = TIME_STEP * vel_r[...]
        else:
            for c in range(3):
                vel[c] = vel[c] + TIME_STEP * (big_f[c] * minv[...])
            vel_r[...] = vel_r[...] + TIME_STEP * (rim_f[...] * minv_r[...])
            disp[...] = disp[...] + TIME_STEP * vel[...]
            disp_r[...] = disp_r[...] + TIME_STEP * vel_r[...]

    rim_value = vel_r[...]
    for c in range(3):
        mean, _, _ = corners(vel, rim_value, c)
        mean = 0.125 * (mean[1:] + mean[:-1])
        for i in range(cx):
            vout_ref[c, :, i, :] = mean[i, 0:cy, :]
    s = stress_of(0.25 * mod[steps - 1])
    for c in range(6):
        for i in range(cx):
            sout_ref[c, :, i, :] = s[c][i, 0:cy, :]


def per_device(stiffness, density, load, alive, surf_coords, surf_nodes, routes, pairs):
    cx, cy, cz = stiffness.shape
    steps = alive.shape[0]
    sb = surf_coords.shape[0]
    npair = pairs.shape[2]
    count_x, count_y, nz = (lax.axis_size(a) for a in ("gx", "gy", "gz"))
    cap = max(sb // 4, sb // nz)
    nx = cx + 1
    pairt = jnp.transpose(pairs[:, 0], (0, 2, 1))
    sizes = (count_x, count_y, cx, cy, cz, sb, npair, steps, nz, cap)
    nslots = nz * cap
    vm = lambda *shape: pltpu.VMEM(shape, F32)
    vh = lambda *shape: pltpu.VMEM(shape, BF16)
    dma = lambda *shape: pltpu.SemaphoreType.DMA(shape)
    column = max(nz - 1, 1)
    scratch = [
        vm(cy, cx, cz), vm(cy, cx, cz), vm(3, cy, cx, cz), pltpu.VMEM((steps, cy, cx, cz), jnp.int32), dma(4),
        vm(steps + 4, cx, 16, cz), vm(4, nx, 16, cz), vm(16, cz), vm(4, nx, 16, cz), vm(16, cz),
        vm(3, nx, 16, cz), vm(16, cz), vm(3, nx, 16, cz), vm(16, cz), vm(nx, 16, cz), vm(16, cz),
        pltpu.VMEM((nz, 8, 128), jnp.int32), vm(steps - 1, nz, sb, 384), vm(3, nslots, 128),
        vm(nslots * 16, 128), vh(nslots, FEATURES, 128), vh(nslots, 128, FEATURES), vh(nslots, 16, 128),
        vm(4 * npair, 128), vm(steps, nz, 8, 384), vm(steps, nz, 8, 384), vm(steps, sb, 128), vm(steps, nslots, 128), vh(steps, 4 * nslots, 4 * npair), vm(nz, 8, 128),
        vh(sb, cx * cy // 2, 128), vh(sb, 2 * cz, 128), vh(sb * 128, 2 * cz), vm(3 * cx * cy, cz), vm(3 * cx * cy, cz),
        vh(sb, 3 * cx * cy, 128),
        vm(steps, 2, 5, 16, cz), vm(steps, 2, 5, 16, cz), vm(steps, 2, 40, cz), vm(steps, 2, 40, cz),
        vm(steps, 2, 2, 8, cz), vm(steps, 2, 2, 8, cz),
        vm(steps, 2, 16, cz), vm(steps, 2, 16, cz), vm(steps, 2, 2, 16, cz), vm(steps, 2, 2, 1, cz), vm(steps, 2, 2, 3, 1, cz),
        dma(column), dma(column), dma(steps - 1, column), dma(steps - 1, column), dma(steps, column), dma(steps, column),
        dma(steps, 26), dma(steps, 26),
    ]
    vmem = pl.BlockSpec(memory_space=pltpu.VMEM)
    vel, stress = pl.pallas_call(
        functools.partial(body, sizes),
        out_shape=(pltpu.VMEM((3, cy, cx, cz), F32), pltpu.VMEM((6, cy, cx, cz), F32)),
        in_specs=[pl.BlockSpec(memory_space=pltpu.MemorySpace.HBM)] * 4 + [vmem] * 4 + [pl.BlockSpec(memory_space=pltpu.SMEM)],
        out_specs=(vmem, vmem),
        scratch_shapes=scratch,
        compiler_params=pltpu.CompilerParams(collective_id=0, has_side_effects=True, vmem_limit_bytes=56 * 1024 * 1024),
    )(jnp.swapaxes(stiffness, 0, 1), jnp.swapaxes(density, 0, 1), jnp.swapaxes(load, 1, 2), jnp.swapaxes(alive, 1, 2),
      jnp.swapaxes(surf_coords, 0, 1), surf_nodes, routes, pairt, pairt)
    return jnp.swapaxes(vel, 1, 2), jnp.swapaxes(stress, 1, 2)


def solution(mesh):
    return jax.shard_map(
        per_device,
        mesh=mesh,
        in_specs=(
            P("gx", "gy", "gz"),
            P("gx", "gy", "gz"),
            P(None, "gx", "gy", "gz"),
            P(None, "gx", "gy", "gz"),
            P(("gx", "gy", "gz"), None, None),
            P(("gx", "gy", "gz"), None),
            P(None, ("gx", "gy", "gz")),
            P(None, ("gx", "gy", "gz"), None, None),
        ),
        out_specs=(P(None, "gx", "gy", "gz"), P(None, "gx", "gy", "gz")),
        check_vma=False,
    )
```

```python
import functools
import itertools
import math

import jax
import jax.numpy as jnp
from jax import lax
from jax.experimental import pallas as pl
from jax.experimental.pallas import tpu as pltpu
from jax.sharding import PartitionSpec as P

REPULSION = 1.0
KERNEL_SCALE = 0.08
TIME_STEP = 0.2
HIGHEST = lax.Precision.HIGHEST
MESH = pl.DeviceIdType.MESH
F32 = jnp.float32
BF16 = jnp.bfloat16
STRETCH = math.sqrt(2.0 * math.log2(math.e) / KERNEL_SCALE)
FEATURES = 32


def iota(shape, dim):
    return lax.broadcasted_iota(jnp.int32, shape, dim)


def hdot(a, b):
    return jnp.dot(a, b, preferred_element_type=F32, precision=HIGHEST)


def split2(x):
    high = x.astype(BF16)
    return high, (x - high.astype(F32)).astype(BF16)


def split3(x):
    high = x.astype(BF16).astype(F32)
    rest = x - high
    middle = rest.astype(BF16).astype(F32)
    return high, middle, rest - middle


def bdot(a, b):
    return jnp.dot(a, b, preferred_element_type=F32)


def sum_x(q):
    return jnp.concatenate([q[:1], q[:-1] + q[1:], q[-1:]], axis=0)


def diff_x(q):
    return jnp.concatenate([-q[:1], q[:-1] - q[1:], q[-1:]], axis=0)


def body(sizes, stiff_hbm, dens_hbm, load_hbm, alive_hbm, coords_hbm, nodes_hbm, routes_hbm, pairt_hbm,
         vout_ref, sout_ref, *scratch):
    (coords_ref, nodes_ref, routes_ref, pairt_ref, pair_ref, early_sem,
     stiff_ref, dens_ref, load_ref, alive_ref, in_sem, mod, big_f, rim_f, load_f, load_r, vel, vel_r, disp, disp_r, minv, minv_r, route_all, pos_all, slots, parts, take_a, turned_b, give_b,
     partial, send_f, ret, back_pick, choose, pair_hot, rank_in, row_pick, lane_pick, lane_turn, flat, touch, scatter_l,
     x_send, x_recv, y_send, y_recv, edge_send, edge_recv, z_send, z_recv, zx_recv, line_send, line_recv,
     route_ss, route_rs, pos_ss, pos_rs, ret_ss, ret_rs, halo_ss, halo_rs) = scratch
    count_x, count_y, cx, cy, cz, sb, npair, steps, nz, cap = sizes
    nx = cx + 1
    rows = 16
    nslots = nz * cap
    ix, iy, iz = lax.axis_index("gx"), lax.axis_index("gy"), lax.axis_index("gz")
    lanes = iota((rows, cz), 1)
    lane3 = iota((1, 1, cz), 2)

    def roll(v, shift, axis):
        return pltpu.roll(v, shift % v.shape[axis], axis)

    inputs = [pltpu.make_async_copy(a, b, in_sem.at[k]) for k, (a, b) in enumerate((
        (stiff_hbm, stiff_ref), (alive_hbm, alive_ref), (load_hbm, load_ref), (dens_hbm, dens_ref)))]
    tables = [pltpu.make_async_copy(a, b, early_sem.at[k]) for k, (a, b) in enumerate((
        (coords_hbm, coords_ref), (routes_hbm, routes_ref), (nodes_hbm, nodes_ref), (pairt_hbm, pairt_ref), (pairt_hbm, pair_ref)))]
    for c in tables + inputs:
        c.start()

    def clear(*refs):
        for ref in refs:
            ref[...] = jnp.zeros(ref.shape, ref.dtype)

    clear(x_recv, y_recv, edge_recv, z_recv, zx_recv, line_recv)

    sides = (("gx", ix, count_x), ("gy", iy, count_y), ("gz", iz, nz))
    only_z = nz == 2
    ways = sorted((d for d in itertools.product((-1, 0, 1), repeat=3) if any(d) and not (only_z and d[2] < 0)), key=lambda d: (-abs(d[2]), -sum(map(abs, d))))

    def there(d, sign):
        return functools.reduce(jnp.logical_and, [
            (at + sign * step >= 0) & (at + sign * step < count)
            for step, (name, at, count) in zip(d, sides) if step and not (only_z and name == "gz")] or [jnp.bool_(True)])

    def neighbor(d):
        return {name: 1 - at if only_z and name == "gz" else at + step for step, (name, at, _) in zip(d, sides) if step}

    sends = [there(d, 1) for d in ways]
    gets = [there(d, -1) for d in ways]
    barrier = pltpu.get_barrier_semaphore()
    expect = jnp.int32(0)
    for d, here in zip(ways, sends):
        @pl.when(here)
        def _():
            pl.semaphore_signal(barrier, inc=1, device_id=neighbor(d), device_id_type=MESH)
        expect = expect + jnp.where(here, 1, 0)
    for other in (range(1, nz) if nz > 2 else ()):
        far = lax.rem(iz + other, nz)
        apart = jnp.logical_and(far != iz - 1, far != iz + 1)

        @pl.when(apart)
        def _():
            pl.semaphore_signal(barrier, inc=1, device_id={"gz": far}, device_id_type=MESH)
        expect = expect + jnp.where(apart, 1, 0)
    for c in tables:
        c.wait()
    pl.semaphore_wait(barrier, expect)

    def column(send_ref, recv_ref, ss, rs):
        out = []
        for other in range(1, nz):
            to = lax.rem(iz + other, nz)
            out.append(pltpu.make_async_remote_copy(
                src_ref=send_ref(to), dst_ref=recv_ref, send_sem=ss.at[other - 1], recv_sem=rs.at[other - 1],
                device_id={"gz": to}, device_id_type=MESH))
        return out

    def pos_copies(phase):
        return column(lambda to: pos_all.at[phase, iz], pos_all.at[phase, iz], pos_ss.at[phase], pos_rs.at[phase])

    def ret_copies(t):
        return column(lambda to: send_f.at[t, to], ret.at[t, iz], ret_ss.at[t], ret_rs.at[t])

    route_copies = column(lambda to: route_all.at[iz], route_all.at[iz], route_ss, route_rs)

    route_all[iz] = jnp.full((8, 128), -1, jnp.int32)
    route_all[iz, 0:steps, 0:sb] = routes_ref[...]
    for x in range(3):
        pos_all[0, iz, :, x * 128:(x + 1) * 128] = coords_ref[x]
    for c in route_copies + pos_copies(0):
        c.start()

    clear(mod, parts, send_f, y_send)
    for c in inputs:
        c.wait()
    for t in range(steps):
        for i in range(cx):
            mod[t, i, 0:cy, :] = stiff_ref[:, i, :] * alive_ref[t, :, i, :].astype(F32)
    for c in range(4):
        for i in range(cx):
            mod[steps + c, i, 0:cy, :] = 0.125 * (load_ref[c, :, i, :] if c < 3 else dens_ref[:, i, :])
    rim = jnp.zeros((rows, cz), F32)
    for c in range(4):
        q = sum_x(mod[steps + c])
        q = q + roll(q, 1, 1)
        r = roll(q, 1, 2)
        load_f[c] = q + jnp.where(lane3 > 0, r, 0.0)
        for i in range(nx):
            at = c * nx + i
            rim = rim + jnp.where(lanes == at, roll(r[i], at, 1), 0.0)
    load_r[...] = rim

    ids = nodes_ref[...]
    row = lax.shift_right_logical(ids, jnp.full(ids.shape, cz.bit_length() - 1, jnp.int32))
    lane = ids & (cz - 1)
    grid_rows = cx * cy
    half_rows = grid_rows // 2
    row2 = lax.shift_right_logical(row, jnp.ones(row.shape, jnp.int32))
    lane2 = lane + (row & 1) * cz
    lane_t = jnp.transpose(jnp.concatenate([lane2.astype(F32), jnp.zeros((128 - sb, 128), F32)], axis=0))
    for s in range(sb):
        row_pick[s] = (iota((half_rows, 128), 0) == row2[s:s + 1, :]).astype(F32).astype(BF16)
        hot = (iota((cz, 128), 0) == lane[s:s + 1, :]).astype(F32).astype(BF16)
        lane_pick[s, 0:cz, :] = hot
        lane_pick[s, cz:2 * cz, :] = hot
        col = jnp.broadcast_to(lane_t[:, s:s + 1], (128, 2 * cz))
        lane_turn[s * 128:(s + 1) * 128, :] = (iota((128, 2 * cz), 1).astype(F32) == col).astype(F32).astype(BF16)

    def wait_all(copies):
        for c in copies:
            c.wait()

    wait_all(route_copies)
    upper = (iota((128, 128), 0) <= iota((128, 128), 1)).astype(F32)
    own = route_all[iz]
    for b in range(nz):
        hits = (route_all[b] == iz).astype(F32)
        rank_in[b] = jnp.where(hits > 0, jnp.dot(hits, upper, preferred_element_type=F32), 0.0)
    slot8 = nz * 8
    picks = []
    for b in range(nz):
        hits = (own == b).astype(F32)
        picks.append(jnp.where(hits > 0, jnp.dot(hits, upper, preferred_element_type=F32), 0.0))
    ranks8 = (iota((8, 128), 0) + 1).astype(F32)
    live8 = iota((8, 128), 0) < cap
    wide = 4 * npair
    spread4 = (lax.shift_right_logical(iota((npair, wide), 1), jnp.full((npair, wide), 2, jnp.int32))
               == iota((npair, wide), 0)).astype(F32)
    for t in range(steps):
        rows_ = [jnp.where((picks[b][t:t + 1, :] == ranks8) & live8, 1.0, 0.0) for b in range(nz)]
        table = jnp.concatenate(rows_ + [jnp.zeros((128 - slot8, 128), F32)], axis=0)
        back_pick[t] = jnp.transpose(table)[0:sb, :]
        hots = [jnp.where(rank_in[b, t:t + 1, :] == ranks8[0:cap], 1.0, 0.0) for b in range(nz)]
        table = jnp.concatenate([roll(hots[b], b * sb, 1) for b in range(nz)], axis=0)
        choose[t] = table
        live = jnp.sum(table, axis=1, keepdims=True)
        pair4 = bdot(pairt_ref[t].astype(F32), spread4)
        slot = iota((nslots, wide), 0).astype(F32)
        is_first = pair4[0:1, :] == slot
        both = (jnp.sum(jnp.where(is_first, live, 0.0), axis=0, keepdims=True)
                * jnp.sum(jnp.where(pair4[1:2, :] == slot, live, 0.0), axis=0, keepdims=True))
        hot = jnp.where(is_first, both, 0.0)
        part = iota((nslots, wide), 1) & 3
        for c in range(4):
            pair_hot[t, c * nslots:(c + 1) * nslots, :] = jnp.where(part == c, hot, 0.0).astype(BF16)

    at8 = iota((8, 128), 0)
    upper_half = at8 < 4
    last = (at8 & 3) == 3
    blank = jnp.zeros((8, 128), F32)

    def put(at, value):
        parts[pl.ds(at, nslots, stride=16), :] = value

    def gather(phase):
        for c in range(3):
            for i in range(cx):
                flat[c * grid_rows + i * cy:c * grid_rows + (i + 1) * cy, :] = disp[c, i, 0:cy, :]
        high, low = split2(flat[...])
        left = jnp.concatenate([high, low], axis=1)
        for s in range(0, sb, 2):
            got = bdot(left, jnp.concatenate([lane_pick[s], lane_pick[s + 1]], axis=1))
            for h in range(2):
                mask = iota((grid_rows, 128), 0) == row[s + h:s + h + 1, :]
                for c in range(3):
                    part = jnp.where(mask, got[c * grid_rows:(c + 1) * grid_rows, h * 128:(h + 1) * 128], 0.0)
                    pos_all[phase, iz, s + h:s + h + 1, c * 128:(c + 1) * 128] = (
                        jnp.sum(part, axis=0, keepdims=True) + coords_ref[c, s + h:s + h + 1, :])

    def build_slots(t, phase):
        pieces = split3(STRETCH * pos_all[phase].reshape(nz * sb, 384))
        got = bdot(choose[t, :, 0:nz * sb].astype(BF16), jnp.concatenate([p.astype(BF16) for p in pieces], axis=1))
        norm = jnp.zeros((nslots, 128), F32)
        for c in range(3):
            high, middle, low = (got[:, k * 384 + c * 128:k * 384 + (c + 1) * 128] for k in range(3))
            x = high + middle + low
            slots[c] = x
            norm = norm - 0.5 * (x * x)
            for k, value in enumerate((high, middle, low)):
                put(4 * k + c, value)
        for k, value in enumerate(split3(norm)):
            put(4 * k + 3, value)
        for k in range(nslots):
            main = parts[k * 16:k * 16 + 8, :]
            rest = parts[k * 16 + 8:k * 16 + 16, :]
            swapped = roll(main, 4, 0)
            ones_b = jnp.where(last, 1.0, main)
            tile_b = [main, jnp.where(upper_half, rest, jnp.where(at8 == 7, 1.0, swapped)), ones_b, blank]
            tile_a = [jnp.where(last, 1.0, jnp.where(upper_half, main, swapped)), jnp.where(at8 == 3, 1.0, main),
                      jnp.where(upper_half, rest, jnp.where(at8 == 7, swapped, main)), blank]
            give = [jnp.where(at8 == 7, 0.0, ones_b), jnp.where(at8 < 3, rest, 0.0)]
            take_a[k] = jnp.concatenate(tile_a, axis=0).astype(BF16)
            give_b[k] = jnp.concatenate(give, axis=0).astype(BF16)
            turned_b[k] = jnp.transpose(jnp.concatenate(tile_b, axis=0)).astype(BF16)


    def pair_range(t, start, stop):
        count = stop - start

        def weigh(q):
            p = pair_ref[t, 0, q]
            r = pair_ref[t, 1, q]
            return bdot(turned_b[r], take_a[p]), give_b[r]

        def gain(exponent, give):
            high, low = split2(jnp.exp2(exponent))
            out = bdot(jnp.concatenate([give, give], axis=1), jnp.concatenate([high, low], axis=0))
            out = out[0:8] + out[8:16]
            return out + roll(out, 4, 0)

        def some(at, carry):
            first = start + at * count
            ahead = weigh(first)
            for u in range(0, count, 2):
                both = []
                for k in (u, u + 1):
                    now, ahead = ahead, weigh(first + k + 1) if k + 1 < count else None
                    both.append(gain(*now))
                partial[pl.ds(pl.multiple_of((first + u) * 4, 8), 8), :] = jnp.where(upper_half, *both)
            return carry

        lax.fori_loop(0, 1 + jnp.minimum(iz, 0), some, 0)

    def finish_pairs(t):
        total = jnp.zeros((4 * nslots, 128), F32)
        for piece in split3(partial[...]):
            total = total + bdot(pair_hot[t], piece.astype(BF16))
        weight = total[3 * nslots:4 * nslots]
        for c in range(3):
            force = (slots[c] * weight - total[c * nslots:(c + 1) * nslots]) * (REPULSION / STRETCH)
            for b in range(nz):
                send_f[t, b, 0:cap, c * 128:(c + 1) * 128] = force[b * cap:(b + 1) * cap]
        for c in ret_copies(t):
            c.start()
        ret[t, iz] = send_f[t, iz]

    def scatter(t):
        halves = split2(ret[t].reshape(slot8, 384))
        force = bdot(back_pick[t, :, 0:slot8].astype(BF16), jnp.concatenate(halves, axis=1))
        for s in range(sb):
            for h in range(2):
                for c in range(3):
                    at = h * 384 + c * 128
                    line = jnp.broadcast_to(force[s:s + 1, at:at + 128], (16, 128)).astype(BF16)
                    spread = row_pick[s].reshape(half_rows // 16, 16, 128) * line[None]
                    at = (3 * h + c) * half_rows
                    scatter_l[s, at:at + half_rows, :] = spread.reshape(half_rows, 128)
        left = jnp.concatenate([scatter_l[s] for s in range(sb)], axis=1)
        total = bdot(left, lane_turn[...])
        total = total[0:3 * half_rows] + total[3 * half_rows:]
        for odd in range(2):
            touch[pl.ds(odd, 3 * half_rows, stride=2), :] = total[:, odd * cz:(odd + 1) * cz]

    def corners(field, rim_value, c):
        u = field[c]
        edge = jnp.stack([roll(rim_value, -(c * nx + i), 1) for i in range(nx)])
        above = roll(jnp.where(lane3 == 0, edge, u), -1, 2)
        both = u + above
        step = above - u
        shifted = roll(both, -1, 1)
        return both + shifted, shifted - both, step + roll(step, -1, 1)

    def stress_of(modulus):
        grads = []
        rim_value = disp_r[...]
        for c in range(3):
            mean, along_y, along_z = corners(disp, rim_value, c)
            grads.append((mean[1:] - mean[:-1], along_y[1:] + along_y[:-1], along_z[1:] + along_z[:-1]))
        trace = grads[0][0] + grads[1][1] + grads[2][2]
        return (modulus * (2.0 * grads[0][0] + trace), modulus * (2.0 * grads[1][1] + trace),
                modulus * (2.0 * grads[2][2] + trace), modulus * (grads[0][1] + grads[1][0]),
                modulus * (grads[1][2] + grads[2][1]), modulus * (grads[0][2] + grads[2][0]))

    def internal(t):
        s = stress_of(-0.0625 * mod[t])
        table = ((s[0], s[3], s[5]), (s[3], s[1], s[4]), (s[5], s[4], s[2]))
        rim = load_r[...]
        for c in range(3):
            a0 = diff_x(table[c][0])
            ay = sum_x(table[c][1])
            az = sum_x(table[c][2])
            a = (a0 - ay) + roll(a0 + ay, 1, 1)
            b = az + roll(az, 1, 1)
            r = roll(a + b, 1, 2)
            big_f[c] = load_f[c] + (a - b) + jnp.where(lane3 > 0, r, 0.0)
            for i in range(nx):
                at = c * nx + i
                rim = rim + jnp.where(lanes == at, roll(r[i], at, 1), 0.0)
        rim_f[...] = rim

    line_lanes = iota((1, cz), 1)
    row_at = iota((rows, cz), 0)

    def halo_copies(t, comps, used):
        out = []
        for n, d in enumerate(ways):
            wx, wy, wz = (0 if step < 0 else 1 for step in d)
            dx, dy, dz = d
            if only_z:
                wz = 1 - iz
            if dz and dy:
                pair = line_send.at[t, wz, wy], line_recv.at[t, wz, wy, dx + 1]
            elif dz and dx:
                pair = z_send.at[t, wz], zx_recv.at[t, wz, wx]
            elif dz:
                pair = z_send.at[t, wz], z_recv.at[t, wz]
            elif dx and dy:
                pair = edge_send.at[t, wx, wy], edge_recv.at[t, wx, wy]
            elif dx:
                pair = x_send.at[t, wx, 0:comps + 1], x_recv.at[t, wx, 0:comps + 1]
            else:
                pair = y_send.at[t, wy, 0:used], y_recv.at[t, wy, 0:used]
            out.append(pltpu.make_async_remote_copy(
                src_ref=pair[0], dst_ref=pair[1], send_sem=halo_ss.at[t, n], recv_sem=halo_rs.at[t, n],
                device_id=neighbor(d), device_id_type=MESH))
        return out

    def halo(t, filler):
        comps = 4 if t == 0 else 3
        used = -(-(1 + comps * nx) // 8) * 8
        lines = ((0, 0), (1, cy))
        packed = jnp.zeros((rows, cz), F32)
        for c in range(comps):
            for i in range(nx):
                at = c * nx + i
                packed = jnp.where(lanes == at, roll(big_f[c, i], at, 1), packed)
        z_send[t, 0] = packed
        z_send[t, 1] = rim_f[...]
        for wy, line in lines:
            line_send[t, 0, wy] = packed[line:line + 1]
            line_send[t, 1, wy] = rim_f[line:line + 1]
        copies = list(zip(ways, halo_copies(t, comps, used), sends, gets))
        along_z = [m[1:] for m in copies if m[0][2]]
        in_plane = [m[1:] for m in copies if not m[0][2]]

        def begin(messages):
            for copy, here, _ in messages:
                @pl.when(here)
                def _():
                    copy.start()

        def end(messages):
            for copy, here, back in messages:
                @pl.when(here)
                def _():
                    copy.wait_send()

                @pl.when(back)
                def _():
                    copy.wait_recv()

        begin(along_z)
        for wx, plane in ((0, 0), (1, cx)):
            x_send[t, wx, 0] = rim_f[...]
            for c in range(comps):
                x_send[t, wx, 1 + c] = big_f[c, plane]
            for wy, line in lines:
                edge_send[t, wx, wy, 0:1] = rim_f[line:line + 1]
                for c in range(comps):
                    edge_send[t, wx, wy, 1 + c:2 + c] = big_f[c, plane, line:line + 1]
        for wy, line in lines:
            y_send[t, wy, 0:1] = rim_f[line:line + 1]
            for c in range(comps):
                for i in range(nx):
                    at = 1 + c * nx + i
                    y_send[t, wy, at:at + 1] = big_f[c, i, line:line + 1]
        begin(in_plane)
        filler()
        end(in_plane)

        def across(tile, wx):
            at = line_lanes if tile.shape[0] == 1 else lanes
            mine = functools.reduce(jnp.logical_or, [at == c * nx + (0 if wx else cx) for c in range(comps)])
            return jnp.where(mine, roll(tile, -cx if wx else cx, 1), 0.0)

        def fold(base, faces, edges, corners_):
            for wx in range(2):
                base = base + across(faces[wx], wx)
            for wy, line in ((1, 0), (0, cy)):
                value = edges[wy] + across(corners_[0][wy], 0) + across(corners_[1][wy], 1)
                base = base + jnp.where(row_at == line, value, 0.0)
            return base

        rim_f[...] = fold(
            rim_f[...], [x_recv[t, wx, 0] for wx in range(2)], [y_recv[t, wy, 0:1] for wy in range(2)],
            [[edge_recv[t, wx, wy, 0:1] for wy in range(2)] for wx in range(2)])
        for c in range(comps):
            big_f[c, 0] = big_f[c, 0] + x_recv[t, 1, 1 + c]
            big_f[c, cx] = big_f[c, cx] + x_recv[t, 0, 1 + c]
        for wy, line in ((1, 0), (0, cy)):
            for c in range(comps):
                for i in range(nx):
                    at = 1 + c * nx + i
                    add = y_recv[t, wy, at:at + 1]
                    if i in (0, cx):
                        wx = 1 if i == 0 else 0
                        add = add + edge_recv[t, wx, wy, 1 + c:2 + c]
                    big_f[c, i, line:line + 1] = big_f[c, i, line:line + 1] + add

        end(along_z)
        folded = [fold(z_recv[t, w], [zx_recv[t, w, wx] for wx in range(2)], [line_recv[t, w, wy, 1] for wy in range(2)],
                       [[line_recv[t, w, wy, 2 * wx] for wy in range(2)] for wx in range(2)]) for w in range(2)]
        rim_f[...] = rim_f[...] + folded[0]
        for c in range(comps):
            for i in range(nx):
                at = c * nx + i
                big_f[c, i] = big_f[c, i] + jnp.where(lanes == 0, roll(folded[1], -at, 1), 0.0)

    def contact(t, phase):
        if phase > 0:
            wait_all(pos_copies(phase))
            build_slots(t, phase)
            pair_range(t, 0, npair)
        finish_pairs(t)

    wait_all(pos_copies(0))
    build_slots(0, 0)
    pair_range(0, 0, npair)
    finish_pairs(0)
    build_slots(1, 0)
    pair_range(1, 0, npair)

    for t in range(steps):
        if t == 0:
            big_f[...] = load_f[...]
            rim_f[...] = load_r[...]
            wait_all(ret_copies(t))
        else:
            if t + 1 < steps:
                gather(t)
                for c in pos_copies(t):
                    c.start()
            wait_all(ret_copies(t))
            internal(t)
        scatter(t)
        for c in range(3):
            for i in range(cx):
                at = c * grid_rows + i * cy
                big_f[c, i, 0:cy, :] = big_f[c, i, 0:cy, :] + touch[at:at + cy, :]
        halo(t, functools.partial(contact, t + 1, t) if t + 1 < steps else lambda: None)
        if t == 0:
            mass = big_f[3]
            minv[...] = jnp.where(mass > 0.0, 1.0 / mass, 0.0)
            held = jnp.where((lanes >= 3 * nx) & (lanes < 4 * nx), rim_f[...], 0.0)
            spread = roll(held, -3 * nx, 1) + roll(held, -2 * nx, 1) + roll(held, -nx, 1)
            minv_r[...] = jnp.where(spread > 0.0, 1.0 / spread, 0.0)
            for c in range(3):
                vel[c] = TIME_STEP * (big_f[c] * minv[...])
            vel_r[...] = TIME_STEP * (rim_f[...] * minv_r[...])
            disp[...] = TIME_STEP * vel[...]
            disp_r[...] = TIME_STEP * vel_r[...]
        else:
            for c in range(3):
                vel[c] = vel[c] + TIME_STEP * (big_f[c] * minv[...])
            vel_r[...] = vel_r[...] + TIME_STEP * (rim_f[...] * minv_r[...])
            disp[...] = disp[...] + TIME_STEP * vel[...]
            disp_r[...] = disp_r[...] + TIME_STEP * vel_r[...]

    rim_value = vel_r[...]
    for c in range(3):
        mean, _, _ = corners(vel, rim_value, c)
        mean = 0.125 * (mean[1:] + mean[:-1])
        for i in range(cx):
            vout_ref[c, :, i, :] = mean[i, 0:cy, :]
    s = stress_of(0.25 * mod[steps - 1])
    for c in range(6):
        for i in range(cx):
            sout_ref[c, :, i, :] = s[c][i, 0:cy, :]


def per_device(stiffness, density, load, alive, surf_coords, surf_nodes, routes, pairs):
    cx, cy, cz = stiffness.shape
    steps = alive.shape[0]
    sb = surf_coords.shape[0]
    npair = pairs.shape[2]
    count_x, count_y, nz = (lax.axis_size(a) for a in ("gx", "gy", "gz"))
    cap = max(sb // 4, sb // nz)
    nx = cx + 1
    pairt = jnp.transpose(pairs[:, 0], (0, 2, 1))
    sizes = (count_x, count_y, cx, cy, cz, sb, npair, steps, nz, cap)
    nslots = nz * cap
    vm = lambda *shape: pltpu.VMEM(shape, F32)
    vh = lambda *shape: pltpu.VMEM(shape, BF16)
    dma = lambda *shape: pltpu.SemaphoreType.DMA(shape)
    column = max(nz - 1, 1)
    scratch = [
        vm(3, sb, 128), pltpu.VMEM((sb, 128), jnp.int32), pltpu.VMEM((steps, sb), jnp.int32),
        pltpu.VMEM((steps, 2, npair), jnp.int32), pltpu.SMEM((steps, 2, npair), jnp.int32), dma(5),
        vm(cy, cx, cz), vm(cy, cx, cz), vm(3, cy, cx, cz), pltpu.VMEM((steps, cy, cx, cz), jnp.int32), dma(4),
        vm(steps + 4, cx, 16, cz), vm(4, nx, 16, cz), vm(16, cz), vm(4, nx, 16, cz), vm(16, cz),
        vm(3, nx, 16, cz), vm(16, cz), vm(3, nx, 16, cz), vm(16, cz), vm(nx, 16, cz), vm(16, cz),
        pltpu.VMEM((nz, 8, 128), jnp.int32), vm(steps - 1, nz, sb, 384), vm(3, nslots, 128),
        vm(nslots * 16, 128), vh(nslots, FEATURES, 128), vh(nslots, 128, FEATURES), vh(nslots, 16, 128),
        vm(4 * npair, 128), vm(steps, nz, 8, 384), vm(steps, nz, 8, 384), vm(steps, sb, 128), vm(steps, nslots, 128), vh(steps, 4 * nslots, 4 * npair), vm(nz, 8, 128),
        vh(sb, cx * cy // 2, 128), vh(sb, 2 * cz, 128), vh(sb * 128, 2 * cz), vm(3 * cx * cy, cz), vm(3 * cx * cy, cz),
        vh(sb, 3 * cx * cy, 128),
        vm(steps, 2, 5, 16, cz), vm(steps, 2, 5, 16, cz), vm(steps, 2, 40, cz), vm(steps, 2, 40, cz),
        vm(steps, 2, 2, 8, cz), vm(steps, 2, 2, 8, cz),
        vm(steps, 2, 16, cz), vm(steps, 2, 16, cz), vm(steps, 2, 2, 16, cz), vm(steps, 2, 2, 1, cz), vm(steps, 2, 2, 3, 1, cz),
        dma(column), dma(column), dma(steps - 1, column), dma(steps - 1, column), dma(steps, column), dma(steps, column),
        dma(steps, 26), dma(steps, 26),
    ]
    vmem = pl.BlockSpec(memory_space=pltpu.VMEM)
    vel, stress = pl.pallas_call(
        functools.partial(body, sizes),
        out_shape=(pltpu.VMEM((3, cy, cx, cz), F32), pltpu.VMEM((6, cy, cx, cz), F32)),
        in_specs=[pl.BlockSpec(memory_space=pltpu.MemorySpace.HBM)] * 8,
        out_specs=(vmem, vmem),
        scratch_shapes=scratch,
        compiler_params=pltpu.CompilerParams(collective_id=0, has_side_effects=True, vmem_limit_bytes=56 * 1024 * 1024),
    )(jnp.swapaxes(stiffness, 0, 1), jnp.swapaxes(density, 0, 1), jnp.swapaxes(load, 1, 2), jnp.swapaxes(alive, 1, 2),
      jnp.swapaxes(surf_coords, 0, 1), surf_nodes, routes, pairt)
    return jnp.swapaxes(vel, 1, 2), jnp.swapaxes(stress, 1, 2)


def solution(mesh):
    return jax.shard_map(
        per_device,
        mesh=mesh,
        in_specs=(
            P("gx", "gy", "gz"),
            P("gx", "gy", "gz"),
            P(None, "gx", "gy", "gz"),
            P(None, "gx", "gy", "gz"),
            P(("gx", "gy", "gz"), None, None),
            P(("gx", "gy", "gz"), None),
            P(None, ("gx", "gy", "gz")),
            P(None, ("gx", "gy", "gz"), None, None),
        ),
        out_specs=(P(None, "gx", "gy", "gz"), P(None, "gx", "gy", "gz")),
        check_vma=False,
    )
```

```python
import functools
import itertools
import math

import jax
import jax.numpy as jnp
from jax import lax
from jax.experimental import pallas as pl
from jax.experimental.pallas import tpu as pltpu
from jax.sharding import PartitionSpec as P

REPULSION = 1.0
KERNEL_SCALE = 0.08
TIME_STEP = 0.2
HIGHEST = lax.Precision.HIGHEST
MESH = pl.DeviceIdType.MESH
F32 = jnp.float32
BF16 = jnp.bfloat16
STRETCH = math.sqrt(2.0 * math.log2(math.e) / KERNEL_SCALE)
FEATURES = 32


def iota(shape, dim):
    return lax.broadcasted_iota(jnp.int32, shape, dim)


def hdot(a, b):
    return jnp.dot(a, b, preferred_element_type=F32, precision=HIGHEST)


def split2(x):
    high = x.astype(BF16)
    return high, (x - high.astype(F32)).astype(BF16)


def split3(x):
    high = x.astype(BF16).astype(F32)
    rest = x - high
    middle = rest.astype(BF16).astype(F32)
    return high, middle, rest - middle


def bdot(a, b):
    return jnp.dot(a, b, preferred_element_type=F32)


def sum_x(q):
    return jnp.concatenate([q[:1], q[:-1] + q[1:], q[-1:]], axis=0)


def diff_x(q):
    return jnp.concatenate([-q[:1], q[:-1] - q[1:], q[-1:]], axis=0)


def body(sizes, stiff_hbm, dens_hbm, load_hbm, alive_hbm, coords_hbm, nodes_hbm, routes_hbm, pairt_hbm,
         vout_ref, sout_ref, *scratch):
    (coords_ref, nodes_ref, routes_ref, pairt_ref, pair_ref, early_sem,
     stiff_ref, dens_ref, load_ref, alive_ref, in_sem, mod, big_f, rim_f, load_f, load_r, vel, vel_r, disp, disp_r, minv, minv_r, route_all, pos_all, slots, parts, take_a, turned_b, give_b,
     partial, send_f, ret, back_pick, choose, pair_hot, rank_in, row_pick, lane_pick, lane_turn, flat, touch, scatter_l,
     x_send, x_recv, y_send, y_recv, edge_send, edge_recv, z_send, z_recv, zx_recv, line_send, line_recv,
     route_ss, route_rs, pos_ss, pos_rs, ret_ss, ret_rs, halo_ss, halo_rs) = scratch
    count_x, count_y, cx, cy, cz, sb, npair, steps, nz, cap = sizes
    nx = cx + 1
    rows = 16
    nslots = nz * cap
    ix, iy, iz = lax.axis_index("gx"), lax.axis_index("gy"), lax.axis_index("gz")
    lanes = iota((rows, cz), 1)
    lane3 = iota((1, 1, cz), 2)

    def roll(v, shift, axis):
        return pltpu.roll(v, shift % v.shape[axis], axis)

    inputs = [pltpu.make_async_copy(a, b, in_sem.at[k]) for k, (a, b) in enumerate((
        (stiff_hbm, stiff_ref), (alive_hbm, alive_ref), (load_hbm, load_ref), (dens_hbm, dens_ref)))]
    tables = [pltpu.make_async_copy(a, b, early_sem.at[k]) for k, (a, b) in enumerate((
        (coords_hbm, coords_ref), (routes_hbm, routes_ref), (nodes_hbm, nodes_ref), (pairt_hbm, pairt_ref), (pairt_hbm, pair_ref)))]
    for c in tables + inputs:
        c.start()

    def clear(*refs):
        for ref in refs:
            ref[...] = jnp.zeros(ref.shape, ref.dtype)

    clear(x_recv, y_recv, edge_recv, z_recv, zx_recv, line_recv)

    sides = (("gx", ix, count_x), ("gy", iy, count_y), ("gz", iz, nz))
    only_z = nz == 2
    ways = sorted((d for d in itertools.product((-1, 0, 1), repeat=3) if any(d) and not (only_z and d[2] < 0)), key=lambda d: (-abs(d[2]), -sum(map(abs, d))))

    def there(d, sign):
        return functools.reduce(jnp.logical_and, [
            (at + sign * step >= 0) & (at + sign * step < count)
            for step, (name, at, count) in zip(d, sides) if step and not (only_z and name == "gz")] or [jnp.bool_(True)])

    def neighbor(d):
        return {name: 1 - at if only_z and name == "gz" else at + step for step, (name, at, _) in zip(d, sides) if step}

    sends = [there(d, 1) for d in ways]
    gets = [there(d, -1) for d in ways]
    barrier = pltpu.get_barrier_semaphore()
    expect = jnp.int32(0)
    for d, here in zip(ways, sends):
        @pl.when(here)
        def _():
            pl.semaphore_signal(barrier, inc=1, device_id=neighbor(d), device_id_type=MESH)
        expect = expect + jnp.where(here, 1, 0)
    for other in (range(1, nz) if nz > 2 else ()):
        far = lax.rem(iz + other, nz)
        apart = jnp.logical_and(far != iz - 1, far != iz + 1)

        @pl.when(apart)
        def _():
            pl.semaphore_signal(barrier, inc=1, device_id={"gz": far}, device_id_type=MESH)
        expect = expect + jnp.where(apart, 1, 0)
    for c in tables:
        c.wait()
    pl.semaphore_wait(barrier, expect)

    def column(send_ref, recv_ref, ss, rs):
        out = []
        for other in range(1, nz):
            to = lax.rem(iz + other, nz)
            out.append(pltpu.make_async_remote_copy(
                src_ref=send_ref(to), dst_ref=recv_ref, send_sem=ss.at[other - 1], recv_sem=rs.at[other - 1],
                device_id={"gz": to}, device_id_type=MESH))
        return out

    def pos_copies(phase):
        return column(lambda to: pos_all.at[phase, iz], pos_all.at[phase, iz], pos_ss.at[phase], pos_rs.at[phase])

    def ret_copies(t):
        return column(lambda to: send_f.at[t, to], ret.at[t, iz], ret_ss.at[t], ret_rs.at[t])

    route_copies = column(lambda to: route_all.at[iz], route_all.at[iz], route_ss, route_rs)

    route_all[iz] = jnp.full((8, 128), -1, jnp.int32)
    route_all[iz, 0:steps, 0:sb] = routes_ref[...]
    for x in range(3):
        pos_all[0, iz, :, x * 128:(x + 1) * 128] = coords_ref[x]
    for c in route_copies + pos_copies(0):
        c.start()

    clear(mod, parts, send_f, y_send)
    for c in inputs:
        c.wait()
    for t in range(steps):
        for i in range(cx):
            mod[t, i, 0:cy, :] = stiff_ref[:, i, :] * alive_ref[t, :, i, :].astype(F32)
    for c in range(4):
        for i in range(cx):
            mod[steps + c, i, 0:cy, :] = 0.125 * (load_ref[c, :, i, :] if c < 3 else dens_ref[:, i, :])
    rim = jnp.zeros((rows, cz), F32)
    for c in range(4):
        q = sum_x(mod[steps + c])
        q = q + roll(q, 1, 1)
        r = roll(q, 1, 2)
        load_f[c] = q + jnp.where(lane3 > 0, r, 0.0)
        for i in range(nx):
            at = c * nx + i
            rim = rim + jnp.where(lanes == at, roll(r[i], at, 1), 0.0)
    load_r[...] = rim

    ids = nodes_ref[...]
    row = lax.shift_right_logical(ids, jnp.full(ids.shape, cz.bit_length() - 1, jnp.int32))
    lane = ids & (cz - 1)
    grid_rows = cx * cy
    half_rows = grid_rows // 2
    row2 = lax.shift_right_logical(row, jnp.ones(row.shape, jnp.int32))
    lane2 = lane + (row & 1) * cz
    lane_t = jnp.transpose(jnp.concatenate([lane2.astype(F32), jnp.zeros((128 - sb, 128), F32)], axis=0))
    for s in range(sb):
        row_pick[s] = (iota((half_rows, 128), 0) == row2[s:s + 1, :]).astype(F32).astype(BF16)
        hot = (iota((cz, 128), 0) == lane[s:s + 1, :]).astype(F32).astype(BF16)
        lane_pick[s, 0:cz, :] = hot
        lane_pick[s, cz:2 * cz, :] = hot
        col = jnp.broadcast_to(lane_t[:, s:s + 1], (128, 2 * cz))
        lane_turn[s * 128:(s + 1) * 128, :] = (iota((128, 2 * cz), 1).astype(F32) == col).astype(F32).astype(BF16)

    def wait_all(copies):
        for c in copies:
            c.wait()

    wait_all(route_copies)
    upper = (iota((128, 128), 0) <= iota((128, 128), 1)).astype(F32)
    own = route_all[iz]
    for b in range(nz):
        hits = (route_all[b] == iz).astype(F32)
        rank_in[b] = jnp.where(hits > 0, jnp.dot(hits, upper, preferred_element_type=F32), 0.0)
    slot8 = nz * 8
    picks = []
    for b in range(nz):
        hits = (own == b).astype(F32)
        picks.append(jnp.where(hits > 0, jnp.dot(hits, upper, preferred_element_type=F32), 0.0))
    ranks8 = (iota((8, 128), 0) + 1).astype(F32)
    live8 = iota((8, 128), 0) < cap
    wide = 4 * npair
    spread4 = (lax.shift_right_logical(iota((npair, wide), 1), jnp.full((npair, wide), 2, jnp.int32))
               == iota((npair, wide), 0)).astype(F32)
    for t in range(steps):
        rows_ = [jnp.where((picks[b][t:t + 1, :] == ranks8) & live8, 1.0, 0.0) for b in range(nz)]
        table = jnp.concatenate(rows_ + [jnp.zeros((128 - slot8, 128), F32)], axis=0)
        back_pick[t] = jnp.transpose(table)[0:sb, :]
        hots = [jnp.where(rank_in[b, t:t + 1, :] == ranks8[0:cap], 1.0, 0.0) for b in range(nz)]
        table = jnp.concatenate([roll(hots[b], b * sb, 1) for b in range(nz)], axis=0)
        choose[t] = table
        live = jnp.sum(table, axis=1, keepdims=True)
        pair4 = bdot(pairt_ref[t].astype(F32), spread4)
        slot = iota((nslots, wide), 0).astype(F32)
        is_first = pair4[0:1, :] == slot
        both = (jnp.sum(jnp.where(is_first, live, 0.0), axis=0, keepdims=True)
                * jnp.sum(jnp.where(pair4[1:2, :] == slot, live, 0.0), axis=0, keepdims=True))
        hot = jnp.where(is_first, both, 0.0)
        part = iota((nslots, wide), 1) & 3
        for c in range(4):
            pair_hot[t, c * nslots:(c + 1) * nslots, :] = jnp.where(part == c, hot, 0.0).astype(BF16)

    at8 = iota((8, 128), 0)
    upper_half = at8 < 4
    last = (at8 & 3) == 3
    blank = jnp.zeros((8, 128), F32)

    def put(at, value):
        parts[pl.ds(at, nslots, stride=16), :] = value

    def gather(phase):
        for c in range(3):
            for i in range(cx):
                flat[c * grid_rows + i * cy:c * grid_rows + (i + 1) * cy, :] = disp[c, i, 0:cy, :]
        high, low = split2(flat[...])
        left = jnp.concatenate([high, low], axis=1)
        for s in range(0, sb, 2):
            got = bdot(left, jnp.concatenate([lane_pick[s], lane_pick[s + 1]], axis=1))
            for h in range(2):
                mask = iota((grid_rows, 128), 0) == row[s + h:s + h + 1, :]
                for c in range(3):
                    part = jnp.where(mask, got[c * grid_rows:(c + 1) * grid_rows, h * 128:(h + 1) * 128], 0.0)
                    pos_all[phase, iz, s + h:s + h + 1, c * 128:(c + 1) * 128] = (
                        jnp.sum(part, axis=0, keepdims=True) + coords_ref[c, s + h:s + h + 1, :])

    def build_slots(t, phase):
        pieces = split3(STRETCH * pos_all[phase].reshape(nz * sb, 384))
        got = bdot(choose[t, :, 0:nz * sb].astype(BF16), jnp.concatenate([p.astype(BF16) for p in pieces], axis=1))
        norm = jnp.zeros((nslots, 128), F32)
        for c in range(3):
            high, middle, low = (got[:, k * 384 + c * 128:k * 384 + (c + 1) * 128] for k in range(3))
            x = high + middle + low
            slots[c] = x
            norm = norm - 0.5 * (x * x)
            for k, value in enumerate((high, middle, low)):
                put(4 * k + c, value)
        for k, value in enumerate(split3(norm)):
            put(4 * k + 3, value)
        for k in range(nslots):
            main = parts[k * 16:k * 16 + 8, :]
            rest = parts[k * 16 + 8:k * 16 + 16, :]
            swapped = roll(main, 4, 0)
            ones_b = jnp.where(last, 1.0, main)
            tile_b = [main, jnp.where(upper_half, rest, jnp.where(at8 == 7, 1.0, swapped)), ones_b, blank]
            tile_a = [jnp.where(last, 1.0, jnp.where(upper_half, main, swapped)), jnp.where(at8 == 3, 1.0, main),
                      jnp.where(upper_half, rest, jnp.where(at8 == 7, swapped, main)), blank]
            give = [jnp.where(at8 == 7, 0.0, ones_b), jnp.where(at8 < 3, rest, 0.0)]
            take_a[k] = jnp.concatenate(tile_a, axis=0).astype(BF16)
            give_b[k] = jnp.concatenate(give, axis=0).astype(BF16)
            turned_b[k] = jnp.transpose(jnp.concatenate(tile_b, axis=0)).astype(BF16)


    def pair_range(t, start, stop):
        count = stop - start

        def weigh(q):
            p = pair_ref[t, 0, q]
            r = pair_ref[t, 1, q]
            return bdot(turned_b[r], take_a[p]), give_b[r]

        def gain(exponent, give):
            high, low = split2(jnp.exp2(exponent))
            out = bdot(jnp.concatenate([give, give], axis=1), jnp.concatenate([high, low], axis=0))
            out = out[0:8] + out[8:16]
            return out + roll(out, 4, 0)

        def some(at, carry):
            first = start + at * count
            ahead = weigh(first)
            for u in range(0, count, 2):
                both = []
                for k in (u, u + 1):
                    now, ahead = ahead, weigh(first + k + 1) if k + 1 < count else None
                    both.append(gain(*now))
                partial[pl.ds(pl.multiple_of((first + u) * 4, 8), 8), :] = jnp.where(upper_half, *both)
            return carry

        lax.fori_loop(0, 1 + jnp.minimum(iz, 0), some, 0)

    def finish_pairs(t):
        total = jnp.zeros((4 * nslots, 128), F32)
        for piece in split3(partial[...]):
            total = total + bdot(pair_hot[t], piece.astype(BF16))
        weight = total[3 * nslots:4 * nslots]
        for c in range(3):
            force = (slots[c] * weight - total[c * nslots:(c + 1) * nslots]) * (REPULSION / STRETCH)
            for b in range(nz):
                send_f[t, b, 0:cap, c * 128:(c + 1) * 128] = force[b * cap:(b + 1) * cap]
        for c in ret_copies(t):
            c.start()
        ret[t, iz] = send_f[t, iz]

    def scatter(t):
        halves = split2(ret[t].reshape(slot8, 384))
        force = bdot(back_pick[t, :, 0:slot8].astype(BF16), jnp.concatenate(halves, axis=1))
        for s in range(sb):
            for h in range(2):
                for c in range(3):
                    at = h * 384 + c * 128
                    line = jnp.broadcast_to(force[s:s + 1, at:at + 128], (16, 128)).astype(BF16)
                    spread = row_pick[s].reshape(half_rows // 16, 16, 128) * line[None]
                    at = (3 * h + c) * half_rows
                    scatter_l[s, at:at + half_rows, :] = spread.reshape(half_rows, 128)
        left = jnp.concatenate([scatter_l[s] for s in range(sb)], axis=1)
        total = bdot(left, lane_turn[...])
        total = total[0:3 * half_rows] + total[3 * half_rows:]
        for odd in range(2):
            touch[pl.ds(odd, 3 * half_rows, stride=2), :] = total[:, odd * cz:(odd + 1) * cz]

    def corners(field, rim_value, c):
        u = field[c]
        edge = jnp.stack([roll(rim_value, -(c * nx + i), 1) for i in range(nx)])
        above = roll(jnp.where(lane3 == 0, edge, u), -1, 2)
        both = u + above
        step = above - u
        shifted = roll(both, -1, 1)
        return both + shifted, shifted - both, step + roll(step, -1, 1)

    def stress_of(modulus):
        grads = []
        rim_value = disp_r[...]
        for c in range(3):
            mean, along_y, along_z = corners(disp, rim_value, c)
            grads.append((mean[1:] - mean[:-1], along_y[1:] + along_y[:-1], along_z[1:] + along_z[:-1]))
        trace = grads[0][0] + grads[1][1] + grads[2][2]
        return (modulus * (2.0 * grads[0][0] + trace), modulus * (2.0 * grads[1][1] + trace),
                modulus * (2.0 * grads[2][2] + trace), modulus * (grads[0][1] + grads[1][0]),
                modulus * (grads[1][2] + grads[2][1]), modulus * (grads[0][2] + grads[2][0]))

    def internal(t):
        s = stress_of(-0.0625 * mod[t])
        table = ((s[0], s[3], s[5]), (s[3], s[1], s[4]), (s[5], s[4], s[2]))
        rim = load_r[...]
        for c in range(3):
            a0 = diff_x(table[c][0])
            ay = sum_x(table[c][1])
            az = sum_x(table[c][2])
            a = (a0 - ay) + roll(a0 + ay, 1, 1)
            b = az + roll(az, 1, 1)
            r = roll(a + b, 1, 2)
            big_f[c] = load_f[c] + (a - b) + jnp.where(lane3 > 0, r, 0.0)
            for i in range(nx):
                at = c * nx + i
                rim = rim + jnp.where(lanes == at, roll(r[i], at, 1), 0.0)
        rim_f[...] = rim

    line_lanes = iota((1, cz), 1)
    row_at = iota((rows, cz), 0)

    def halo_copies(t, comps, used):
        out = []
        for n, d in enumerate(ways):
            wx, wy, wz = (0 if step < 0 else 1 for step in d)
            dx, dy, dz = d
            if only_z:
                wz = 1 - iz
            if dz and dy:
                pair = line_send.at[t, wz, wy], line_recv.at[t, wz, wy, dx + 1]
            elif dz and dx:
                pair = z_send.at[t, wz], zx_recv.at[t, wz, wx]
            elif dz:
                pair = z_send.at[t, wz], z_recv.at[t, wz]
            elif dx and dy:
                pair = edge_send.at[t, wx, wy], edge_recv.at[t, wx, wy]
            elif dx:
                pair = x_send.at[t, wx, 0:comps + 1], x_recv.at[t, wx, 0:comps + 1]
            else:
                pair = y_send.at[t, wy, 0:used], y_recv.at[t, wy, 0:used]
            out.append(pltpu.make_async_remote_copy(
                src_ref=pair[0], dst_ref=pair[1], send_sem=halo_ss.at[t, n], recv_sem=halo_rs.at[t, n],
                device_id=neighbor(d), device_id_type=MESH))
        return out

    def halo(t, filler):
        comps = 4 if t == 0 else 3
        used = -(-(1 + comps * nx) // 8) * 8
        lines = ((0, 0), (1, cy))
        packed = jnp.zeros((rows, cz), F32)
        for c in range(comps):
            for i in range(nx):
                at = c * nx + i
                packed = jnp.where(lanes == at, roll(big_f[c, i], at, 1), packed)
        z_send[t, 0] = packed
        z_send[t, 1] = rim_f[...]
        for wy, line in lines:
            line_send[t, 0, wy] = packed[line:line + 1]
            line_send[t, 1, wy] = rim_f[line:line + 1]
        copies = list(zip(ways, halo_copies(t, comps, used), sends, gets))
        along_z = [m[1:] for m in copies if m[0][2]]
        in_plane = [m[1:] for m in copies if not m[0][2]]

        def begin(messages):
            for copy, here, _ in messages:
                @pl.when(here)
                def _():
                    copy.start()

        def end(messages):
            for copy, here, back in messages:
                @pl.when(here)
                def _():
                    copy.wait_send()

                @pl.when(back)
                def _():
                    copy.wait_recv()

        begin(along_z)
        for wx, plane in ((0, 0), (1, cx)):
            x_send[t, wx, 0] = rim_f[...]
            for c in range(comps):
                x_send[t, wx, 1 + c] = big_f[c, plane]
            for wy, line in lines:
                edge_send[t, wx, wy, 0:1] = rim_f[line:line + 1]
                for c in range(comps):
                    edge_send[t, wx, wy, 1 + c:2 + c] = big_f[c, plane, line:line + 1]
        for wy, line in lines:
            y_send[t, wy, 0:1] = rim_f[line:line + 1]
            for c in range(comps):
                for i in range(nx):
                    at = 1 + c * nx + i
                    y_send[t, wy, at:at + 1] = big_f[c, i, line:line + 1]
        begin(in_plane)
        filler()
        end(in_plane)

        def across(tile, wx):
            at = line_lanes if tile.shape[0] == 1 else lanes
            mine = functools.reduce(jnp.logical_or, [at == c * nx + (0 if wx else cx) for c in range(comps)])
            return jnp.where(mine, roll(tile, -cx if wx else cx, 1), 0.0)

        def fold(base, faces, edges, corners_):
            for wx in range(2):
                base = base + across(faces[wx], wx)
            for wy, line in ((1, 0), (0, cy)):
                value = edges[wy] + across(corners_[0][wy], 0) + across(corners_[1][wy], 1)
                base = base + jnp.where(row_at == line, value, 0.0)
            return base

        rim_f[...] = fold(
            rim_f[...], [x_recv[t, wx, 0] for wx in range(2)], [y_recv[t, wy, 0:1] for wy in range(2)],
            [[edge_recv[t, wx, wy, 0:1] for wy in range(2)] for wx in range(2)])
        for c in range(comps):
            big_f[c, 0] = big_f[c, 0] + x_recv[t, 1, 1 + c]
            big_f[c, cx] = big_f[c, cx] + x_recv[t, 0, 1 + c]
        for wy, line in ((1, 0), (0, cy)):
            for c in range(comps):
                for i in range(nx):
                    at = 1 + c * nx + i
                    add = y_recv[t, wy, at:at + 1]
                    if i in (0, cx):
                        wx = 1 if i == 0 else 0
                        add = add + edge_recv[t, wx, wy, 1 + c:2 + c]
                    big_f[c, i, line:line + 1] = big_f[c, i, line:line + 1] + add

        end(along_z)
        folded = [fold(z_recv[t, w], [zx_recv[t, w, wx] for wx in range(2)], [line_recv[t, w, wy, 1] for wy in range(2)],
                       [[line_recv[t, w, wy, 2 * wx] for wy in range(2)] for wx in range(2)]) for w in range(2)]
        rim_f[...] = rim_f[...] + folded[0]
        for c in range(comps):
            for i in range(nx):
                at = c * nx + i
                big_f[c, i] = big_f[c, i] + jnp.where(lanes == 0, roll(folded[1], -at, 1), 0.0)

    def contact(t, phase):
        if phase > 0:
            wait_all(pos_copies(phase))
            build_slots(t, phase)
            pair_range(t, 0, npair)
        finish_pairs(t)

    wait_all(pos_copies(0))
    build_slots(0, 0)
    pair_range(0, 0, npair)
    finish_pairs(0)
    build_slots(1, 0)
    pair_range(1, 0, npair)

    for t in range(steps):
        if t == 0:
            big_f[...] = load_f[...]
            rim_f[...] = load_r[...]
            wait_all(ret_copies(t))
        else:
            if t + 1 < steps:
                gather(t)
                for c in pos_copies(t):
                    c.start()
                internal(t)
                wait_all(ret_copies(t))
            else:
                wait_all(ret_copies(t))
                internal(t)
        scatter(t)
        for c in range(3):
            for i in range(cx):
                at = c * grid_rows + i * cy
                big_f[c, i, 0:cy, :] = big_f[c, i, 0:cy, :] + touch[at:at + cy, :]
        halo(t, functools.partial(contact, t + 1, t) if t + 1 < steps else lambda: None)
        if t == 0:
            mass = big_f[3]
            minv[...] = jnp.where(mass > 0.0, 1.0 / mass, 0.0)
            held = jnp.where((lanes >= 3 * nx) & (lanes < 4 * nx), rim_f[...], 0.0)
            spread = roll(held, -3 * nx, 1) + roll(held, -2 * nx, 1) + roll(held, -nx, 1)
            minv_r[...] = jnp.where(spread > 0.0, 1.0 / spread, 0.0)
            for c in range(3):
                vel[c] = TIME_STEP * (big_f[c] * minv[...])
            vel_r[...] = TIME_STEP * (rim_f[...] * minv_r[...])
            disp[...] = TIME_STEP * vel[...]
            disp_r[...] = TIME_STEP * vel_r[...]
        else:
            for c in range(3):
                vel[c] = vel[c] + TIME_STEP * (big_f[c] * minv[...])
            vel_r[...] = vel_r[...] + TIME_STEP * (rim_f[...] * minv_r[...])
            disp[...] = disp[...] + TIME_STEP * vel[...]
            disp_r[...] = disp_r[...] + TIME_STEP * vel_r[...]

    rim_value = vel_r[...]
    for c in range(3):
        mean, _, _ = corners(vel, rim_value, c)
        mean = 0.125 * (mean[1:] + mean[:-1])
        for i in range(cx):
            vout_ref[c, :, i, :] = mean[i, 0:cy, :]
    s = stress_of(0.25 * mod[steps - 1])
    for c in range(6):
        for i in range(cx):
            sout_ref[c, :, i, :] = s[c][i, 0:cy, :]


def per_device(stiffness, density, load, alive, surf_coords, surf_nodes, routes, pairs):
    cx, cy, cz = stiffness.shape
    steps = alive.shape[0]
    sb = surf_coords.shape[0]
    npair = pairs.shape[2]
    count_x, count_y, nz = (lax.axis_size(a) for a in ("gx", "gy", "gz"))
    cap = max(sb // 4, sb // nz)
    nx = cx + 1
    pairt = jnp.transpose(pairs[:, 0], (0, 2, 1))
    sizes = (count_x, count_y, cx, cy, cz, sb, npair, steps, nz, cap)
    nslots = nz * cap
    vm = lambda *shape: pltpu.VMEM(shape, F32)
    vh = lambda *shape: pltpu.VMEM(shape, BF16)
    dma = lambda *shape: pltpu.SemaphoreType.DMA(shape)
    column = max(nz - 1, 1)
    scratch = [
        vm(3, sb, 128), pltpu.VMEM((sb, 128), jnp.int32), pltpu.VMEM((steps, sb), jnp.int32),
        pltpu.VMEM((steps, 2, npair), jnp.int32), pltpu.SMEM((steps, 2, npair), jnp.int32), dma(5),
        vm(cy, cx, cz), vm(cy, cx, cz), vm(3, cy, cx, cz), pltpu.VMEM((steps, cy, cx, cz), jnp.int32), dma(4),
        vm(steps + 4, cx, 16, cz), vm(4, nx, 16, cz), vm(16, cz), vm(4, nx, 16, cz), vm(16, cz),
        vm(3, nx, 16, cz), vm(16, cz), vm(3, nx, 16, cz), vm(16, cz), vm(nx, 16, cz), vm(16, cz),
        pltpu.VMEM((nz, 8, 128), jnp.int32), vm(steps - 1, nz, sb, 384), vm(3, nslots, 128),
        vm(nslots * 16, 128), vh(nslots, FEATURES, 128), vh(nslots, 128, FEATURES), vh(nslots, 16, 128),
        vm(4 * npair, 128), vm(steps, nz, 8, 384), vm(steps, nz, 8, 384), vm(steps, sb, 128), vm(steps, nslots, 128), vh(steps, 4 * nslots, 4 * npair), vm(nz, 8, 128),
        vh(sb, cx * cy // 2, 128), vh(sb, 2 * cz, 128), vh(sb * 128, 2 * cz), vm(3 * cx * cy, cz), vm(3 * cx * cy, cz),
        vh(sb, 3 * cx * cy, 128),
        vm(steps, 2, 5, 16, cz), vm(steps, 2, 5, 16, cz), vm(steps, 2, 40, cz), vm(steps, 2, 40, cz),
        vm(steps, 2, 2, 8, cz), vm(steps, 2, 2, 8, cz),
        vm(steps, 2, 16, cz), vm(steps, 2, 16, cz), vm(steps, 2, 2, 16, cz), vm(steps, 2, 2, 1, cz), vm(steps, 2, 2, 3, 1, cz),
        dma(column), dma(column), dma(steps - 1, column), dma(steps - 1, column), dma(steps, column), dma(steps, column),
        dma(steps, 26), dma(steps, 26),
    ]
    vmem = pl.BlockSpec(memory_space=pltpu.VMEM)
    vel, stress = pl.pallas_call(
        functools.partial(body, sizes),
        out_shape=(pltpu.VMEM((3, cy, cx, cz), F32), pltpu.VMEM((6, cy, cx, cz), F32)),
        in_specs=[pl.BlockSpec(memory_space=pltpu.MemorySpace.HBM)] * 8,
        out_specs=(vmem, vmem),
        scratch_shapes=scratch,
        compiler_params=pltpu.CompilerParams(collective_id=0, has_side_effects=True, vmem_limit_bytes=56 * 1024 * 1024),
    )(jnp.swapaxes(stiffness, 0, 1), jnp.swapaxes(density, 0, 1), jnp.swapaxes(load, 1, 2), jnp.swapaxes(alive, 1, 2),
      jnp.swapaxes(surf_coords, 0, 1), surf_nodes, routes, pairt)
    return jnp.swapaxes(vel, 1, 2), jnp.swapaxes(stress, 1, 2)


def solution(mesh):
    return jax.shard_map(
        per_device,
        mesh=mesh,
        in_specs=(
            P("gx", "gy", "gz"),
            P("gx", "gy", "gz"),
            P(None, "gx", "gy", "gz"),
            P(None, "gx", "gy", "gz"),
            P(("gx", "gy", "gz"), None, None),
            P(("gx", "gy", "gz"), None),
            P(None, ("gx", "gy", "gz")),
            P(None, ("gx", "gy", "gz"), None, None),
        ),
        out_specs=(P(None, "gx", "gy", "gz"), P(None, "gx", "gy", "gz")),
        check_vma=False,
    )
```
